128 devices in a mesh: row: 8 (over y, x_hi), col: 16 (over z, x_lo, core).
Axes of the slice: x: 4 (x_hi: 2, x_lo: 2; x = x_hi * 2 + x_lo), y: 4, z: 4, core: 2. Of those that a mesh axis runs over, the one named last changes fastest.
Arguments:
- front: float32 [16384, 16384], P('row', 'col'), may hold values from -6 to 6
- pivot: float32 [1024, 1024], P(('row', 'col')), as said below
- panel: float32 [16384, 1024], P(('row', 'col')), may hold values from -4 to 4
- child_blocks: bfloat16 [16384, 128, 128], P(('row', 'col')), may hold values from -6 to 6
- child_dest: int32 [16384, 1], P(('row', 'col')), may hold values from 0 to 127; in each aligned block of 128 rows (0 to 127, 128 to 255, ...) at most 2 rows name the same one
- child_pos: int32 [16384], P(('row', 'col')), may hold values from 0 to 127
- pattern: int32 [128, 128], P('row', 'col'), may hold values 0 or 1
Outputs:
- schur: float32 [16384, 16384], P('row', 'col')
- factor: float32 [16384, 1024], P(('row', 'col'))
The draws below stay inside these ranges and needn't reach their ends.
Inputs may be any that keep to these rules, and one draw needn't show every extreme that they name: pivot is symmetric positive definite. `child_dest`: among the child blocks of one device no owner is named more than 2 times, a bound that some block reaches.
All inputs are finite; a program needn't handle non-finite values. No bound on the sum of `pattern` on one device may be relied on, other than what follows from the above.
Results may differ from the reference program's by a relative error of at most 0.0023.
Values may be sent and summed in bfloat16 or wider, within the bound.
A program may use at most 192 MiB of HBM per device.

```python
import math
import jax
import jax.numpy as jnp
import numpy as np
from jax import lax

ORDER = 16384
PIVOTS = 1024
BLOCK = 128
CB_DEV = 128
CAP = 2
CHILDREN = 16384
NBLK = 128
TILE_BLOCKS = 128
N_ROW = 8
N_COL = 16
DEVICES = 128


def draw_pivot(key, part):
    key_one, key_two = jax.random.split(key, 2)
    noise = jax.random.uniform(key_one, (PIVOTS, PIVOTS), jnp.float32, -1.0, 1.0)
    matrix = (noise + noise.T) * (1.2 / PIVOTS ** 0.5)
    diagonal = jax.random.uniform(key_two, (PIVOTS,), jnp.float32, 2.4, 3.0)
    matrix = matrix + jnp.diag(diagonal)
    return matrix


def plant(entries, own_key, least, high):
    spot = [jax.random.randint(jax.random.fold_in(own_key, axis), (), 0, length) for axis, length in enumerate(entries.shape)]
    main_axis = entries.shape.index(max(entries.shape))
    next_to = spot[:main_axis] + [(spot[main_axis] + 1) % entries.shape[main_axis]] + spot[main_axis + 1:]
    return entries.at[tuple(spot)].set(least).at[tuple(next_to)].set(high)


def block_scale(own_key, dims, pieces, smallest, largest):
    loudness = 1.0
    for position, blocks in pieces:
        steps = jax.random.uniform(jax.random.fold_in(jax.random.fold_in(own_key, 6), position), (blocks,), jnp.float32, smallest / len(pieces), largest / len(pieces))
        loudness = loudness * jnp.repeat(jnp.exp(steps), dims[position] // blocks).reshape((-1,) + (1,) * (len(dims) - 1 - position))
    return loudness


def deal_out(key, own, number, rows, count, top, most, lean):
    ranking = jax.random.permutation(key, count)
    heavy_load, usual = load_shares(count, rows * top, most, lean, True), load_shares(count, rows * top, most, lean, False)
    places = jnp.arange(count)

    def named(lengths, rotation):
        used = int((lengths > 0).sum())
        fixed = max(1, used // 4)
        passed = fixed + (places - fixed + rotation * (used - fixed)) % max(1, count - fixed)
        return jnp.zeros((count,), jnp.int32).at[ranking[jnp.where(places < fixed, places, passed)]].set(jnp.asarray(lengths, jnp.int32))

    lengths = jnp.where(number % 4 == 0, named(heavy_load, number // 4), named(usual, number - number // 4 - 1))
    mixed = jax.random.permutation(jax.random.fold_in(own, 3), count)
    source_of, taker = mixed[0:count // 2 * 2:2], mixed[1:count // 2 * 2:2]
    room = jnp.minimum(lengths[source_of] - 1, most - lengths[taker]) // 2
    room = jnp.where((source_of == ranking[0]) | (taker == ranking[0]) | (lengths[taker] == 0), 0, jnp.maximum(room, 0))
    passed = jax.random.randint(jax.random.fold_in(own, 4), (count // 2,), 0, 1 << 20) % (room + 1)
    lengths = lengths.at[source_of].add(-passed).at[taker].add(passed)
    members = jnp.searchsorted(jnp.cumsum(lengths), jnp.arange(rows * top), side="right").astype(jnp.int32)
    grid = members.reshape(top, rows).T
    grid = grid[jax.random.permutation(jax.random.fold_in(own, 1), rows)]
    rotation = jax.random.randint(jax.random.fold_in(own, 2), (rows, 1), 0, top)
    return jnp.take_along_axis(grid, (jnp.arange(top)[None, :] + rotation) % top, axis=1)


def load_shares(amount, total, bound, lean, full):
    weights = [(1 << 20) // math.isqrt(rank ** lean) + 1 for rank in range(1, amount + 1)]
    largest = bound if full else min(bound, max(-(-total // amount), total * weights[0] // sum(weights)))
    least = 1 if total - largest >= amount - 1 else 0
    holding, spare = [largest] + [least] * (amount - 1), total - largest - least * (amount - 1)
    while spare > 0:
        movable = [i for i in range(1, amount) if holding[i] < largest] or [i for i in range(1, amount) if holding[i] < bound]
        pool, budget = sum([weights[i] for i in movable]), spare
        for i in movable:
            more = min(bound - holding[i], max(1, budget * weights[i] // pool), spare)
            holding[i] = holding[i] + more
            spare = spare - more
    return np.array(holding)


def centred(key, shape, spread, reach, shards=(), dtype=jnp.bfloat16):
    array = jax.random.normal(key, shape, jnp.float32) * spread
    if len(shards) > 0:
        array = block_scale(key, shape, shards, -0.22, 0.18) * array
    return jnp.clip(array, min=-reach, max=reach).astype(dtype)


def setup_inputs(seed: int = 0) -> dict:
    key_list = jax.random.split(jax.random.key(seed), 8)
    front = centred(key_list[0], (ORDER, ORDER), 1.0, 6.0, ((0, 8), (1, 16)), jnp.float32)
    pivot = draw_pivot(jax.random.fold_in(key_list[7], 71), 0)
    panel = centred(key_list[2], (ORDER, PIVOTS), (1.6 / PIVOTS ** 0.25), 4.0, ((0, 128),), jnp.float32)
    child_blocks = centred(key_list[3], (CHILDREN, BLOCK, BLOCK), 1.0, 6.0, ((0, 128),))
    child_dest_keys = jax.random.split(jax.random.fold_in(key_list[4], 1), CHILDREN // CB_DEV)
    child_dest_turns = jax.random.permutation(jax.random.fold_in(key_list[4], 3), CHILDREN // CB_DEV)
    child_dest = jax.vmap(lambda own, number: deal_out(jax.random.fold_in(key_list[4], 2), own, number, CB_DEV, DEVICES, 1, CAP, 2))(child_dest_keys, child_dest_turns).reshape((CHILDREN, 1))
    child_pos = plant(jax.random.randint(key_list[5], (CHILDREN,), 0, TILE_BLOCKS), jax.random.fold_in(key_list[5], 1), 0, TILE_BLOCKS - 1).astype(jnp.int32)
    pattern = plant((jax.random.randint(key_list[6], (NBLK, NBLK), 0, 4) < 3).astype(jnp.int32), jax.random.fold_in(key_list[6], 1), 0, 1)
    return {"front": front, "pivot": pivot, "panel": panel, "child_blocks": child_blocks, "child_dest": child_dest, "child_pos": child_pos, "pattern": pattern}


def reference(front, pivot, panel, child_blocks, child_dest, child_pos, pattern):
    lower_factor = jnp.linalg.cholesky(pivot)
    factor = lax.linalg.triangular_solve(lower_factor, panel, left_side=False, lower=True, transpose_a=True)
    rounded = factor.astype(jnp.bfloat16).astype(jnp.float32)
    tile_row_blocks = ORDER // N_ROW // BLOCK
    tile_col_blocks = ORDER // N_COL // BLOCK
    owner = child_dest[:, 0]
    grid_row = owner // N_COL * tile_row_blocks + child_pos // tile_col_blocks
    grid_col = owner % N_COL * tile_col_blocks + child_pos % tile_col_blocks
    extra = jnp.zeros((NBLK, NBLK, BLOCK, BLOCK), jnp.float32)
    extra = extra.at[grid_row, grid_col].add(child_blocks.astype(jnp.float32))
    extra = extra.transpose(0, 2, 1, 3).reshape(ORDER, ORDER)
    assembled = front + extra
    update = jnp.dot(rounded.astype(jnp.float32), rounded.T.astype(jnp.float32), precision=lax.Precision.HIGHEST, preferred_element_type=jnp.float32)
    masked = update.reshape(NBLK, BLOCK, NBLK, BLOCK) * pattern.astype(jnp.float32)[:, None, :, None]
    schur = assembled - masked.reshape(ORDER, ORDER)
    return (schur, factor)
```

```python
import jax
import jax.numpy as jnp
from jax import lax
from jax.experimental import pallas as pl
from jax.experimental.pallas import tpu as pltpu
from jax.sharding import PartitionSpec as P

SIDE = 128
SUB = 8
HIGHEST = lax.Precision.HIGHEST
MESH = pl.DeviceIdType.MESH
VMEM = pltpu.VMEM
HBM = pltpu.HBM
CONTRACT_LAST = (((1,), (1,)), ((), ()))


def coordinates():
    row, col = lax.axis_index("row"), lax.axis_index("col")
    return {
        "y": row // 2,
        "x": (row % 2) * 2 + (col // 2) % 2,
        "z": col // 4,
        "core": col % 2,
    }


def mesh_index(at):
    return (at["y"] * 2 + at["x"] // 2, at["z"] * 4 + (at["x"] % 2) * 2 + at["core"])


def pack_kernel(dest_ref, blocks_ref, out_ref, count, sem):
    devices = count.shape[0]
    number = blocks_ref.shape[0]

    @pl.loop(0, devices)
    def _(d):
        count[d] = 0

    @pl.loop(0, number)
    def _(i):
        owner = dest_ref[i]
        used = count[owner]
        count[owner] = used + 1
        pltpu.make_async_copy(blocks_ref.at[i], out_ref.at[owner * 2 + used], sem).start()

    pltpu.make_async_copy(blocks_ref, blocks_ref, sem).wait()


def pack(dest, blocks, devices):
    number, side, _ = blocks.shape
    return pl.pallas_call(
        pack_kernel,
        out_shape=jax.ShapeDtypeStruct((2 * devices, side, side), blocks.dtype),
        grid_spec=pltpu.PrefetchScalarGridSpec(
            num_scalar_prefetch=1,
            grid=(),
            in_specs=[pl.BlockSpec(memory_space=VMEM)],
            out_specs=pl.BlockSpec(memory_space=HBM),
            scratch_shapes=[pltpu.SMEM((devices,), jnp.int32), pltpu.SemaphoreType.DMA],
        ),
        name="pack",
    )(dest, blocks)


ORDERS = (("x", "y", "z"), ("y", "z", "x"), ("z", "x", "y"))


def gather_kernel(piece_bounds, own_ref, out_ref, local_sem, send_sem, recv_sem, pair_send, pair_recv):
    me = coordinates()
    pieces = range(len(ORDERS))
    first = {
        "y": me["y"], "xh": me["x"] // 2, "z": me["z"], "xl": me["x"] % 2, "core": me["core"],
    }

    def view(done, piece):
        low, high = piece_bounds[piece]
        pick = lambda name, axis: slice(None) if axis in done else first[name]
        return out_ref.at[
            pick("y", "y"), pick("xh", "x"), pick("z", "z"), pick("xl", "x"), first["core"], :, pl.ds(low, high - low)
        ]

    own = out_ref.at[first["y"], first["xh"], first["z"], first["xl"], first["core"]]
    copy = pltpu.make_async_copy(own_ref, own, local_sem)
    copy.start()

    def send(piece, stage, turn):
        done, axis = ORDERS[piece][:stage], ORDERS[piece][stage]
        at = dict(me)
        at[axis] = jnp.bitwise_xor(me[axis], turn)
        low, high = piece_bounds[piece]
        source = own_ref.at[:, pl.ds(low, high - low)] if stage == 0 else view(done, piece)
        return pltpu.make_async_remote_copy(
            src_ref=source,
            dst_ref=view(done, piece),
            send_sem=send_sem.at[piece, stage, turn - 1],
            recv_sem=recv_sem.at[piece, stage, turn - 1],
            device_id=mesh_index(at),
            device_id_type=MESH,
        )

    def pair(piece, stage):
        at = dict(me)
        at["core"] = 1 - me["core"]
        ref = view(ORDERS[piece][:stage], piece)
        return pltpu.make_async_remote_copy(
            src_ref=ref, dst_ref=ref, send_sem=pair_send.at[piece], recv_sem=pair_recv.at[piece],
            device_id=mesh_index(at), device_id_type=MESH,
        )

    turns = (1, 3, 2)
    for piece in pieces:
        for turn in turns:
            send(piece, 0, turn).start()
    copy.wait()
    for stage in (1, 2):
        for piece in pieces:
            for turn in turns:
                send(piece, stage - 1, turn).wait_recv()
            for turn in turns:
                send(piece, stage, turn).start()
    for piece in pieces:
        for turn in turns:
            send(piece, 2, turn).wait_recv()
        pair(piece, 3).start()
    for piece in pieces:
        for stage in range(3):
            for turn in turns:
                send(piece, stage, turn).wait_send()
        pair(piece, 3).wait()


def gather(own):
    rows, width = own.shape
    third = (width // SIDE // 3) * SIDE
    bounds = ((0, third), (third, 2 * third), (2 * third, width))
    count = len(ORDERS)

    def kernel(*refs):
        gather_kernel(bounds, *refs)

    out = pl.pallas_call(
        kernel,
        out_shape=jax.ShapeDtypeStruct((4, 2, 4, 2, 2, rows, width), own.dtype),
        in_specs=[pl.BlockSpec(memory_space=HBM)],
        out_specs=pl.BlockSpec(memory_space=HBM),
        scratch_shapes=[
            pltpu.SemaphoreType.DMA,
            pltpu.SemaphoreType.DMA((count, 3, 3)),
            pltpu.SemaphoreType.DMA((count, 3, 3)),
            pltpu.SemaphoreType.DMA((count,)),
            pltpu.SemaphoreType.DMA((count,)),
        ],
        compiler_params=pltpu.CompilerParams(has_side_effects=True),
        name="pivot_gather",
    )(own)
    return out.reshape(128 * rows, width)


def factor_block(load, store):
    groups = SIDE // SUB
    block = [load(h) for h in range(groups)]
    rows = lax.broadcasted_iota(jnp.int32, (SUB, SIDE), 0)
    cols = lax.broadcasted_iota(jnp.int32, (SUB, SIDE), 1)
    inverse = [jnp.where(cols == rows + SUB * h, 1.0, 0.0).astype(jnp.float32) for h in range(groups)]

    def spread_row(value, r):
        return jnp.broadcast_to(value[r : r + 1, :], (SUB, SIDE))

    def spread_column(value, c):
        return jnp.broadcast_to(value[:, c : c + 1], (SUB, SIDE))

    for g in range(groups):
        heads = [spread_column(block[g], SUB * g + j) for j in range(SUB)]
        corner = {(i, j): spread_row(heads[j], i) for j in range(SUB) for i in range(j, SUB)}
        upper = [spread_row(block[g], i) for i in range(SUB)]
        lower = [spread_row(inverse[g], i) for i in range(SUB)]
        below = {h: [spread_column(block[h], SUB * g + j) for j in range(SUB)] for h in range(g + 1, groups)}
        for j in range(SUB):
            scale = lax.rsqrt(corner[j, j])
            column = {i: corner[i, j] * scale for i in range(j + 1, SUB)}
            for i in range(j + 1, SUB):
                for k in range(j + 1, i + 1):
                    corner[i, k] = corner[i, k] - column[i] * column[k]
            u = upper[j] * scale
            w = lower[j] * scale
            for i in range(j + 1, SUB):
                upper[i] = upper[i] - column[i] * u
                lower[i] = lower[i] - column[i] * w
            for h in range(g + 1, groups):
                entry = below[h][j] * scale
                for i in range(j + 1, SUB):
                    below[h][i] = below[h][i] - entry * column[i]
                block[h] = block[h] - entry * u
                inverse[h] = inverse[h] - entry * w
            store(SUB * g + j, w[0:1, :])


def cholesky_kernel(pivot_ref, panel_ref, factor_ref, rounded_ref, work, solved, inverse):
    size = factor_ref.shape[1]
    own = panel_ref.shape[0]
    blocks = size // SIDE
    work[pl.ds(0, size), :] = pivot_ref[:, pl.ds(0, size)]
    work[pl.ds(size, own), :] = panel_ref[...]

    @pl.loop(0, blocks)
    def _(k):
        start = pl.multiple_of(k * SIDE, SIDE)
        columns = pl.ds(start, SIDE)

        def load(h):
            return work[pl.ds(pl.multiple_of(start + SUB * h, SUB), SUB), columns]

        def store(r, value):
            inverse[r : r + 1, :] = value

        factor_block(load, store)
        solved[...] = lax.dot_general(
            work[:, columns], inverse[...], CONTRACT_LAST, precision=HIGHEST, preferred_element_type=jnp.float32
        )
        mine = solved[pl.ds(size, own), :]
        factor_ref[:, columns] = mine
        rounded_ref[:, columns] = mine.astype(jnp.bfloat16)

        @pl.loop(k + 1, blocks)
        def _(j):
            there = pl.multiple_of(j * SIDE, SIDE)
            work[:, pl.ds(there, SIDE)] = work[:, pl.ds(there, SIDE)] - lax.dot_general(
                solved[...], solved[pl.ds(there, SIDE), :], CONTRACT_LAST,
                precision=HIGHEST, preferred_element_type=jnp.float32,
            )


def cholesky_solve(pivot, panel):
    own, size = panel.shape
    return pl.pallas_call(
        cholesky_kernel,
        out_shape=(jax.ShapeDtypeStruct((own, size), jnp.float32), jax.ShapeDtypeStruct((own, size), jnp.bfloat16)),
        in_specs=[pl.BlockSpec(memory_space=VMEM)] * 2,
        out_specs=(pl.BlockSpec(memory_space=VMEM),) * 2,
        scratch_shapes=[
            VMEM((size + own, size), jnp.float32), VMEM((size + own, SIDE), jnp.float32), VMEM((SIDE, SIDE), jnp.float32),
        ],
        compiler_params=pltpu.CompilerParams(vmem_limit_bytes=30 << 20),
        cost_estimate=pl.CostEstimate(flops=10**10, bytes_accessed=10**7, transcendentals=0),
        name="cholesky_solve",
    )(pivot, panel)


def spread_kernel(own_ref, row_ref, col_ref, local_sem, row_send, row_recv, pair_send, pair_recv, col_send, col_recv):
    row, col = lax.axis_index("row"), lax.axis_index("col")
    chip, core = col // 2, col % 2
    column = row * 2 + col // 8
    pairs = row_send.shape[0]
    rows = col_send.shape[0]
    local = pltpu.make_async_copy(own_ref, row_ref.at[col], local_sem)
    local.start()

    def along(turn):
        return pltpu.make_async_remote_copy(
            src_ref=own_ref, dst_ref=row_ref.at[col],
            send_sem=row_send.at[turn - 1], recv_sem=row_recv.at[turn - 1],
            device_id=(row, jnp.bitwise_xor(chip, turn) * 2 + core), device_id_type=MESH,
        )

    def pair(turn):
        block = row_ref.at[jnp.bitwise_xor(chip, turn) * 2 + core]
        return pltpu.make_async_remote_copy(
            src_ref=own_ref if turn == 0 else block, dst_ref=block,
            send_sem=pair_send.at[turn], recv_sem=pair_recv.at[turn],
            device_id=(row, chip * 2 + 1 - core), device_id_type=MESH,
        )

    def down(turn):
        return pltpu.make_async_remote_copy(
            src_ref=own_ref, dst_ref=col_ref.at[col % 8],
            send_sem=col_send.at[turn], recv_sem=col_recv.at[col % 8],
            device_id=(jnp.bitwise_xor(row, turn), column), device_id_type=MESH,
        )

    def arrival(k):
        return pltpu.make_async_remote_copy(
            src_ref=own_ref, dst_ref=col_ref.at[k], send_sem=col_send.at[0], recv_sem=col_recv.at[k],
            device_id=(row, col), device_id_type=MESH,
        )

    for turn in range(1, pairs + 1):
        along(turn).start()
        down(turn).start()
    at_home = col == column
    @pl.when(at_home)
    def _():
        pltpu.make_async_copy(own_ref, col_ref.at[col % 8], col_recv.at[col % 8]).start()
    @pl.when(jnp.logical_not(at_home))
    def _():
        down(0).start()
    pair(0).start()
    for turn in range(1, pairs + 1):
        along(turn).wait_recv()
        pair(turn).start()
    for k in range(rows):
        arrival(k).wait_recv()
    local.wait()
    for turn in range(1, pairs + 1):
        along(turn).wait_send()
        down(turn).wait_send()
    @pl.when(jnp.logical_not(at_home))
    def _():
        down(0).wait_send()
    for turn in range(pairs + 1):
        pair(turn).wait()


def spread(rounded):
    own, size = rounded.shape
    cols, rows = lax.axis_size("col"), lax.axis_size("row")
    dma = pltpu.SemaphoreType.DMA
    row_side, col_side = pl.pallas_call(
        spread_kernel,
        out_shape=(
            jax.ShapeDtypeStruct((cols, own, size), rounded.dtype),
            jax.ShapeDtypeStruct((size // own, own, size), rounded.dtype),
        ),
        in_specs=[pl.BlockSpec(memory_space=HBM)],
        out_specs=(pl.BlockSpec(memory_space=HBM),) * 2,
        scratch_shapes=[dma, dma((7,)), dma((7,)), dma((8,)), dma((8,)), dma((rows,)), dma((8,))],
        compiler_params=pltpu.CompilerParams(has_side_effects=True),
        name="factor_spread",
    )(rounded)
    return row_side.reshape(cols * own, size), col_side.reshape(size, size)


def update_kernel(pattern_ref, front_ref, row_ref, col_ref, out_ref):
    step = pl.program_id(0)
    height, width = out_ref.shape
    product = lax.dot_general(row_ref[...], col_ref[...], CONTRACT_LAST, preferred_element_type=jnp.float32)
    for a in range(height // SIDE):
        for b in range(width // SIDE):
            here = (slice(a * SIDE, (a + 1) * SIDE), slice(b * SIDE, (b + 1) * SIDE))
            keep = pattern_ref[step * (height // SIDE) + a, b].astype(jnp.float32)
            out_ref[here] = front_ref[here] - product[here] * keep


def trailing(pattern, front, row_side, col_side):
    tile_rows, tile_cols = front.shape
    size = row_side.shape[1]
    height = 256
    return pl.pallas_call(
        update_kernel,
        out_shape=jax.ShapeDtypeStruct(front.shape, jnp.float32),
        grid_spec=pltpu.PrefetchScalarGridSpec(
            num_scalar_prefetch=1,
            grid=(tile_rows // height,),
            in_specs=[
                pl.BlockSpec((height, tile_cols), lambda i, p: (i, 0)),
                pl.BlockSpec((height, size), lambda i, p: (i, 0)),
                pl.BlockSpec((tile_cols, size), lambda i, p: (0, 0)),
            ],
            out_specs=pl.BlockSpec((height, tile_cols), lambda i, p: (i, 0)),
        ),
        compiler_params=pltpu.CompilerParams(vmem_limit_bytes=30 << 20),
        cost_estimate=pl.CostEstimate(flops=2 * tile_rows * tile_cols * size, bytes_accessed=24 << 20, transcendentals=0),
        name="trailing",
    )(pattern, front, row_side, col_side)


def extend_kernel(place_ref, base_ref, arrived_ref, out_ref, tile, slots, load_sem, slot_sem, out_sem):
    total = arrived_ref.shape[0]
    chunk = slots.shape[1]
    steps = total // chunk
    block_cols = tile.shape[1] // SIDE
    blocks = (tile.shape[0] // SIDE) * block_cols

    def fetch(c):
        return pltpu.make_async_copy(arrived_ref.at[pl.ds(c * chunk, chunk)], slots.at[c % 2], slot_sem.at[c % 2])

    load = pltpu.make_async_copy(base_ref, tile, load_sem)
    load.start()
    fetch(0).start()
    load.wait()
    for c in range(steps):
        if c + 1 < steps:
            fetch(c + 1).start()
        fetch(c).wait()

        @pl.loop(0, chunk)
        def _(n):
            place = place_ref[c * chunk + n]

            @pl.when(place < blocks)
            def _():
                top = pl.multiple_of((place // block_cols) * SIDE, SIDE)
                left = pl.multiple_of((place % block_cols) * SIDE, SIDE)
                here = (pl.ds(top, SIDE), pl.ds(left, SIDE))
                tile[here] = tile[here] + slots[c % 2, n].astype(jnp.float32)

    store = pltpu.make_async_copy(tile, out_ref, out_sem)
    store.start()
    store.wait()


def extend_add(places, base, arrived):
    dma = pltpu.SemaphoreType.DMA
    return pl.pallas_call(
        extend_kernel,
        out_shape=jax.ShapeDtypeStruct(base.shape, base.dtype),
        grid_spec=pltpu.PrefetchScalarGridSpec(
            num_scalar_prefetch=1,
            grid=(),
            in_specs=[pl.BlockSpec(memory_space=HBM)] * 2,
            out_specs=pl.BlockSpec(memory_space=HBM),
            scratch_shapes=[
                VMEM(base.shape, jnp.float32), VMEM((2, 32, SIDE, SIDE), arrived.dtype), dma, dma((2,)), dma,
            ],
        ),
        compiler_params=pltpu.CompilerParams(vmem_limit_bytes=20 << 20),
        name="extend_add",
    )(places, base, arrived)


def arrivals(dest, pos, me, blocks):
    lane = lax.broadcasted_iota(jnp.int32, dest.shape, 1)
    mine = dest == me
    first = jnp.min(jnp.where(mine, lane, dest.shape[1]), axis=1)
    last = jnp.max(jnp.where(mine, lane, -1), axis=1)
    place_first = jnp.sum(jnp.where(lane == first[:, None], pos, 0), axis=1)
    place_last = jnp.sum(jnp.where(lane == last[:, None], pos, 0), axis=1)
    place_first = jnp.where(last >= 0, place_first, blocks)
    place_last = jnp.where(last > first, place_last, blocks)
    return jnp.stack([place_first, place_last], axis=1).reshape(-1)


def per_device(front, pivot, panel, child_blocks, child_dest, child_pos, pattern):
    devices = lax.axis_size("row") * lax.axis_size("col")
    me = lax.axis_index("row") * lax.axis_size("col") + lax.axis_index("col")
    size = panel.shape[1]
    dest = child_dest[:, 0]
    outgoing = pack(dest, child_blocks, devices)
    arrived = lax.all_to_all(outgoing, ("row", "col"), split_axis=0, concat_axis=0, tiled=True)
    notes = jnp.concatenate([dest[None], child_pos[None], jnp.zeros((6, dest.shape[0]), jnp.int32)], axis=0)
    everything = gather(jnp.concatenate([pivot, notes.astype(jnp.float32)], axis=1))
    factor, rounded = cholesky_solve(everything, panel)
    row_side, col_side = spread(rounded)
    base = trailing(pattern, front, row_side, col_side)
    told = everything[:, size:].reshape(devices, 8, -1).astype(jnp.int32)
    tile_blocks = (front.shape[0] // SIDE) * (front.shape[1] // SIDE)
    places = arrivals(told[:, 0], told[:, 1], me, tile_blocks)
    schur = extend_add(places, base, arrived)
    return (schur, factor)


def solution(mesh):
    return jax.shard_map(
        per_device,
        mesh=mesh,
        in_specs=(
            P("row", "col"),
            P(("row", "col"), None),
            P(("row", "col"), None),
            P(("row", "col"), None, None),
            P(("row", "col"), None),
            P(("row", "col")),
            P("row", "col"),
        ),
        out_specs=(P("row", "col"), P(("row", "col"), None)),
        check_vma=False,
    )
```

```python
import jax
import jax.numpy as jnp
from jax import lax
from jax.experimental import pallas as pl
from jax.experimental.pallas import tpu as pltpu
from jax.sharding import PartitionSpec as P

SIDE = 128
SUB = 8
HIGHEST = lax.Precision.HIGHEST
MESH = pl.DeviceIdType.MESH
VMEM = pltpu.VMEM
HBM = pltpu.HBM
CONTRACT_LAST = (((1,), (1,)), ((), ()))


def coordinates():
    row, col = lax.axis_index("row"), lax.axis_index("col")
    return {
        "y": row // 2,
        "x": (row % 2) * 2 + (col // 2) % 2,
        "z": col // 4,
        "core": col % 2,
    }


def mesh_index(at):
    return (at["y"] * 2 + at["x"] // 2, at["z"] * 4 + (at["x"] % 2) * 2 + at["core"])


def pack_kernel(dest_ref, blocks_ref, out_ref, count, sem):
    devices = count.shape[0]
    number = blocks_ref.shape[0]

    @pl.loop(0, devices)
    def _(d):
        count[d] = 0

    @pl.loop(0, number)
    def _(i):
        owner = dest_ref[i]
        used = count[owner]
        count[owner] = used + 1
        pltpu.make_async_copy(blocks_ref.at[i], out_ref.at[owner * 2 + used], sem).start()

    pltpu.make_async_copy(blocks_ref, blocks_ref, sem).wait()


def pack(dest, blocks, devices):
    number, side, _ = blocks.shape
    return pl.pallas_call(
        pack_kernel,
        out_shape=jax.ShapeDtypeStruct((2 * devices, side, side), blocks.dtype),
        grid_spec=pltpu.PrefetchScalarGridSpec(
            num_scalar_prefetch=1,
            grid=(),
            in_specs=[pl.BlockSpec(memory_space=VMEM)],
            out_specs=pl.BlockSpec(memory_space=HBM),
            scratch_shapes=[pltpu.SMEM((devices,), jnp.int32), pltpu.SemaphoreType.DMA],
        ),
        name="pack",
    )(dest, blocks)


ORDERS = (("x", "y", "z"), ("y", "z", "x"), ("z", "x", "y"))
RING = 4


def gather_kernel(piece_bounds, own_ref, out_ref, local_sem, send_sem, recv_sem, ring_send, ring_recv, pair_send, pair_recv):
    me = coordinates()
    pieces = range(len(ORDERS))

    def view(piece, done, at, part=None):
        low, high = piece_bounds[piece] if part is None else part
        pick = lambda value, axis: slice(None) if axis in done else value
        return out_ref.at[
            pick(at["y"], "y"), pick(at["x"] // 2, "x"), pick(at["z"], "z"), pick(at["x"] % 2, "x"), me["core"],
            :, pl.ds(low, high - low),
        ]

    def moved(axis, value):
        at = dict(me)
        at[axis] = value
        return at

    copy = pltpu.make_async_copy(own_ref, out_ref.at[me["y"], me["x"] // 2, me["z"], me["x"] % 2, me["core"]], local_sem)
    copy.start()

    def send(piece, stage, turn):
        done, axis = ORDERS[piece][:stage], ORDERS[piece][stage]
        low, high = piece_bounds[piece]
        there = view(piece, done, me)
        return pltpu.make_async_remote_copy(
            src_ref=own_ref.at[:, pl.ds(low, high - low)] if stage == 0 else there,
            dst_ref=there,
            send_sem=send_sem.at[piece, stage, turn - 1],
            recv_sem=recv_sem.at[piece, stage, turn - 1],
            device_id=mesh_index(moved(axis, jnp.bitwise_xor(me[axis], turn))),
            device_id_type=MESH,
        )

    def ring(piece, step):
        done, axis = ORDERS[piece][:2], ORDERS[piece][2]
        low, high = piece_bounds[piece]
        cut = low + ((high - low) // SIDE * 2 // 3) * SIDE
        up, down = (me[axis] + 1) % RING, (me[axis] + RING - 1) % RING
        origin, target, part = (
            (me[axis], up, (low, high)), (me[axis], down, (low, high)), (down, up, (low, cut)), (up, down, (cut, high)),
        )[step]
        ref = view(piece, done, moved(axis, origin), part)
        return pltpu.make_async_remote_copy(
            src_ref=ref, dst_ref=ref, send_sem=ring_send.at[piece, step], recv_sem=ring_recv.at[piece, step],
            device_id=mesh_index(moved(axis, target)), device_id_type=MESH,
        )

    def pair(piece, step):
        done, axis = ORDERS[piece][:2], ORDERS[piece][2]
        ref = view(piece, done, moved(axis, (me[axis] + (0, RING - 1, 1, 2)[step]) % RING))
        return pltpu.make_async_remote_copy(
            src_ref=ref, dst_ref=ref, send_sem=pair_send.at[piece, step], recv_sem=pair_recv.at[piece, step],
            device_id=mesh_index(moved("core", 1 - me["core"])), device_id_type=MESH,
        )

    turns = (1, 3, 2)
    for piece in pieces:
        for turn in turns:
            send(piece, 0, turn).start()
    copy.wait()
    for piece in pieces:
        for turn in turns:
            send(piece, 0, turn).wait_recv()
        for turn in turns:
            send(piece, 1, turn).start()
    for piece in pieces:
        for turn in turns:
            send(piece, 1, turn).wait_recv()
        ring(piece, 0).start()
        ring(piece, 1).start()
        pair(piece, 0).start()
    for piece in pieces:
        for step in (0, 1):
            ring(piece, step).wait_recv()
            ring(piece, step + 2).start()
            pair(piece, step + 1).start()
    for piece in pieces:
        ring(piece, 2).wait_recv()
        ring(piece, 3).wait_recv()
        pair(piece, 3).start()
    for piece in pieces:
        for turn in turns:
            send(piece, 0, turn).wait_send()
            send(piece, 1, turn).wait_send()
        for step in range(4):
            ring(piece, step).wait_send()
            pair(piece, step).wait()


def gather(own):
    rows, width = own.shape
    third = (width // SIDE // 3) * SIDE
    bounds = ((0, third), (third, 2 * third), (2 * third, width))
    count = len(ORDERS)
    dma = pltpu.SemaphoreType.DMA

    def kernel(*refs):
        gather_kernel(bounds, *refs)

    out = pl.pallas_call(
        kernel,
        out_shape=jax.ShapeDtypeStruct((4, 2, 4, 2, 2, rows, width), own.dtype),
        in_specs=[pl.BlockSpec(memory_space=HBM)],
        out_specs=pl.BlockSpec(memory_space=HBM),
        scratch_shapes=[
            dma, dma((count, 2, 3)), dma((count, 2, 3)), dma((count, 4)), dma((count, 4)), dma((count, 4)), dma((count, 4)),
        ],
        compiler_params=pltpu.CompilerParams(has_side_effects=True),
        name="pivot_gather",
    )(own)
    return out.reshape(128 * rows, width)


def factor_block(load, store):
    groups = SIDE // SUB
    block = [load(h) for h in range(groups)]
    rows = lax.broadcasted_iota(jnp.int32, (SUB, SIDE), 0)
    cols = lax.broadcasted_iota(jnp.int32, (SUB, SIDE), 1)
    inverse = [jnp.where(cols == rows + SUB * h, 1.0, 0.0).astype(jnp.float32) for h in range(groups)]

    def spread_row(value, r):
        return jnp.broadcast_to(value[r : r + 1, :], (SUB, SIDE))

    def spread_column(value, c):
        return jnp.broadcast_to(value[:, c : c + 1], (SUB, SIDE))

    for g in range(groups):
        heads = [spread_column(block[g], SUB * g + j) for j in range(SUB)]
        corner = {(i, j): spread_row(heads[j], i) for j in range(SUB) for i in range(j, SUB)}
        upper = [spread_row(block[g], i) for i in range(SUB)]
        lower = [spread_row(inverse[g], i) for i in range(SUB)]
        below = {h: [spread_column(block[h], SUB * g + j) for j in range(SUB)] for h in range(g + 1, groups)}
        for j in range(SUB):
            scale = lax.rsqrt(corner[j, j])
            column = {i: corner[i, j] * scale for i in range(j + 1, SUB)}
            for i in range(j + 1, SUB):
                for k in range(j + 1, i + 1):
                    corner[i, k] = corner[i, k] - column[i] * column[k]
            u = upper[j] * scale
            w = lower[j] * scale
            for i in range(j + 1, SUB):
                upper[i] = upper[i] - column[i] * u
                lower[i] = lower[i] - column[i] * w
            for h in range(g + 1, groups):
                entry = below[h][j] * scale
                for i in range(j + 1, SUB):
                    below[h][i] = below[h][i] - entry * column[i]
                block[h] = block[h] - entry * u
                inverse[h] = inverse[h] - entry * w
            store(SUB * g + j, w[0:1, :])


def cholesky_kernel(pivot_ref, panel_ref, factor_ref, rounded_ref, work, solved, inverse):
    size = factor_ref.shape[1]
    own = panel_ref.shape[0]
    blocks = size // SIDE
    work[pl.ds(0, size), :] = pivot_ref[:, pl.ds(0, size)]
    work[pl.ds(size, own), :] = panel_ref[...]

    @pl.loop(0, blocks)
    def _(k):
        start = pl.multiple_of(k * SIDE, SIDE)
        columns = pl.ds(start, SIDE)

        def load(h):
            return work[pl.ds(pl.multiple_of(start + SUB * h, SUB), SUB), columns]

        def store(r, value):
            inverse[r : r + 1, :] = value

        factor_block(load, store)
        solved[...] = lax.dot_general(
            work[:, columns], inverse[...], CONTRACT_LAST, precision=HIGHEST, preferred_element_type=jnp.float32
        )
        mine = solved[pl.ds(size, own), :]
        factor_ref[:, columns] = mine
        rounded_ref[:, columns] = mine.astype(jnp.bfloat16)

        @pl.loop(k + 1, blocks)
        def _(j):
            there = pl.multiple_of(j * SIDE, SIDE)
            work[:, pl.ds(there, SIDE)] = work[:, pl.ds(there, SIDE)] - lax.dot_general(
                solved[...], solved[pl.ds(there, SIDE), :], CONTRACT_LAST,
                precision=HIGHEST, preferred_element_type=jnp.float32,
            )


def cholesky_solve(pivot, panel):
    own, size = panel.shape
    return pl.pallas_call(
        cholesky_kernel,
        out_shape=(jax.ShapeDtypeStruct((own, size), jnp.float32), jax.ShapeDtypeStruct((own, size), jnp.bfloat16)),
        in_specs=[pl.BlockSpec(memory_space=VMEM)] * 2,
        out_specs=(pl.BlockSpec(memory_space=VMEM),) * 2,
        scratch_shapes=[
            VMEM((size + own, size), jnp.float32), VMEM((size + own, SIDE), jnp.float32), VMEM((SIDE, SIDE), jnp.float32),
        ],
        compiler_params=pltpu.CompilerParams(vmem_limit_bytes=30 << 20),
        cost_estimate=pl.CostEstimate(flops=10**10, bytes_accessed=10**7, transcendentals=0),
        name="cholesky_solve",
    )(pivot, panel)


def spread_kernel(
    own_ref, row_ref, col_ref, local_sem, turn_send, turn_recv, send_sem, recv_sem, pair_send, pair_recv,
):
    me = coordinates()
    core = me["core"]
    row, chip = lax.axis_index("row"), lax.axis_index("col") // 2
    half = own_ref.shape[1] // 2
    sides = (
        (row_ref, "z", me["x"] % 2, lambda flip: me["x"] // 2 * 2 + flip),
        (col_ref, "y", me["x"] // 2, lambda flip: flip * 2 + me["x"] % 2),
    )

    def moved(axis, value):
        at = dict(me)
        at[axis] = value
        return mesh_index(at)

    def block(side, place, flip):
        ref, _, mine, _ = sides[side]
        return ref.at[place, jnp.bitwise_xor(mine, flip), core]

    def send(side, step):
        _, axis, mine, place_x = sides[side]
        here = me[axis]
        up, down = (here + 1) % RING, (here + RING - 1) % RING
        if step == 0:
            origin, flip, part, target = here, 0, None, moved("x", place_x(1 - mine))
        elif step < 5:
            flip = (step - 1) // 2
            origin, part, target = here, None, moved(axis, (up, down)[(step - 1) % 2])
        else:
            flip = (step - 5) // 2
            way = (step - 5) % 2
            origin, part, target = (down, up)[way], way * half, moved(axis, (up, down)[way])
        ref = block(side, origin, flip)
        if part is not None:
            ref = ref.at[:, pl.ds(part, half)]
        source = own_ref if side == 0 and step in (0, 1, 2) else ref
        return pltpu.make_async_remote_copy(
            src_ref=source, dst_ref=ref, send_sem=send_sem.at[side, step], recv_sem=recv_sem.at[side, step],
            device_id=target, device_id_type=MESH,
        )

    def pair(side, shift, flip):
        place = (me[sides[side][1]] + shift) % RING
        ref = block(side, place, flip)
        go = pltpu.make_async_remote_copy(
            src_ref=own_ref if side == 0 and shift == 0 and flip == 0 else ref, dst_ref=ref,
            send_sem=pair_send.at[side], recv_sem=pair_recv.at[side],
            device_id=moved("core", 1 - core), device_id_type=MESH,
        )
        if side == 0:
            go.start()
        else:
            @pl.when(place // 2 != core)
            def _():
                go.start()

    first = row_ref.at[me["z"], me["x"] % 2, core]
    local = pltpu.make_async_copy(own_ref, first, local_sem.at[0])
    local.start()
    turned = col_ref.at[chip // 2, chip % 2, core]
    turn = pltpu.make_async_remote_copy(
        src_ref=own_ref, dst_ref=turned, send_sem=turn_send, recv_sem=turn_recv,
        device_id=(chip, row * 2 + core), device_id_type=MESH,
    )
    stay = pltpu.make_async_copy(own_ref, turned, local_sem.at[1])
    at_home = row == chip

    @pl.when(at_home)
    def _():
        stay.start()

    @pl.when(jnp.logical_not(at_home))
    def _():
        turn.start()

    for step in (0, 1, 2):
        send(0, step).start()
    pair(0, 0, 0)

    @pl.when(at_home)
    def _():
        stay.wait()

    @pl.when(jnp.logical_not(at_home))
    def _():
        turn.wait_recv()

    for step in (0, 1, 2):
        send(1, step).start()
    pair(1, 0, 0)
    for side in (0, 1):
        send(side, 0).wait_recv()
        send(side, 3).start()
        send(side, 4).start()
        pair(side, 0, 1)
    for flip in (0, 1):
        for way in (0, 1):
            for side in (0, 1):
                send(side, 1 + 2 * flip + way).wait_recv()
                send(side, 5 + 2 * flip + way).start()
                pair(side, (RING - 1, 1)[way], flip)
    for flip in (0, 1):
        for side in (0, 1):
            for way in (0, 1):
                send(side, 5 + 2 * flip + way).wait_recv()
            pair(side, 2, flip)
    local.wait()

    @pl.when(jnp.logical_not(at_home))
    def _():
        turn.wait_send()

    for side in (0, 1):
        for step in range(9):
            send(side, step).wait_send()
        ref = sides[side][0].at[pl.ds(0, RING if side == 0 else 2), :, 0]
        whole = pltpu.make_async_remote_copy(
            src_ref=ref, dst_ref=ref, send_sem=pair_send.at[side], recv_sem=pair_recv.at[side],
            device_id=moved("core", 1 - core), device_id_type=MESH,
        )
        whole.wait()


def spread(rounded):
    own, size = rounded.shape
    dma = pltpu.SemaphoreType.DMA
    side = jax.ShapeDtypeStruct((RING, 2, 2, own, size), rounded.dtype)
    row_side, col_side = pl.pallas_call(
        spread_kernel,
        out_shape=(side, side),
        in_specs=[pl.BlockSpec(memory_space=VMEM)],
        out_specs=(pl.BlockSpec(memory_space=HBM),) * 2,
        scratch_shapes=[dma((2,)), dma, dma, dma((2, 9)), dma((2, 9)), dma((2,)), dma((2,))],
        compiler_params=pltpu.CompilerParams(has_side_effects=True),
        name="factor_spread",
    )(rounded)
    return row_side.reshape(16 * own, size), col_side.reshape(16 * own, size)


def finish_kernel(
    place_ref, pattern_ref, front_ref, arrived_ref, row_ref, col_ref, out_ref,
    tile, slots, rows, cols, load_sem, slot_sem, row_sem, col_sem, out_sem,
):
    total = arrived_ref.shape[0]
    chunk = slots.shape[1]
    steps = total // chunk
    bands = out_sem.shape[0]
    height, width = tile.shape[0] // bands, tile.shape[1]
    block_cols = width // SIDE
    blocks = (tile.shape[0] // SIDE) * block_cols

    def fetch(c):
        return pltpu.make_async_copy(arrived_ref.at[pl.ds(c * chunk, chunk)], slots.at[c % 2], slot_sem.at[c % 2])

    load = pltpu.make_async_copy(front_ref, tile, load_sem)
    load.start()
    fetch(0).start()
    core = lax.axis_index("col") % 2
    half = pl.ds(pl.multiple_of(core * cols.shape[0], SIDE), cols.shape[0])
    load_cols = pltpu.make_async_copy(col_ref.at[half], cols, col_sem)
    load_rows = pltpu.make_async_copy(row_ref, rows, row_sem)
    load.wait()

    for c in range(steps):
        if c + 1 < steps:
            fetch(c + 1).start()
        if c == steps - 3:
            load_cols.start()
            load_rows.start()
        fetch(c).wait()

        @pl.loop(0, chunk)
        def _(n):
            place = place_ref[c * chunk + n]

            @pl.when(place < blocks)
            def _():
                top = pl.multiple_of((place // block_cols) * SIDE, SIDE)
                left = pl.multiple_of((place % block_cols) * SIDE, SIDE)
                here = (pl.ds(top, SIDE), pl.ds(left, SIDE))
                tile[here] = tile[here] + slots[c % 2, n].astype(jnp.float32)

    load_cols.wait()
    load_rows.wait()

    def put(band):
        part = pl.ds(pl.multiple_of(band * height, height), height)
        return pltpu.make_async_copy(tile.at[part], out_ref.at[part], out_sem.at[band])

    @pl.loop(0, bands)
    def _(band):
        low = pl.multiple_of(band * height, height)
        product = lax.dot_general(
            rows[pl.ds(low, height), :], cols[...], CONTRACT_LAST, preferred_element_type=jnp.float32
        )
        for a in range(height // SIDE):
            for b in range(block_cols):
                here = (pl.ds(low + a * SIDE, SIDE), pl.ds(b * SIDE, SIDE))
                keep = pattern_ref[band * (height // SIDE) + a, b].astype(jnp.float32)
                tile[here] = tile[here] - product[a * SIDE : (a + 1) * SIDE, b * SIDE : (b + 1) * SIDE] * keep
        put(band).start()

    @pl.loop(0, bands)
    def _(band):
        put(band).wait()


def finish(places, pattern, front, arrived, row_side, col_side):
    dma = pltpu.SemaphoreType.DMA
    bands = front.shape[0] // 256
    return pl.pallas_call(
        finish_kernel,
        out_shape=jax.ShapeDtypeStruct(front.shape, front.dtype),
        grid_spec=pltpu.PrefetchScalarGridSpec(
            num_scalar_prefetch=2,
            grid=(),
            in_specs=[pl.BlockSpec(memory_space=HBM)] * 4,
            out_specs=pl.BlockSpec(memory_space=HBM),
            scratch_shapes=[
                VMEM(front.shape, jnp.float32), VMEM((2, 32, SIDE, SIDE), arrived.dtype),
                VMEM(row_side.shape, row_side.dtype), VMEM((front.shape[1], col_side.shape[1]), col_side.dtype),
                dma, dma((2,)), dma, dma, dma((bands,)),
            ],
        ),
        compiler_params=pltpu.CompilerParams(vmem_limit_bytes=62 << 20),
        name="finish",
    )(places, pattern, front, arrived, row_side, col_side)


def arrivals(dest, pos, me, blocks):
    lane = lax.broadcasted_iota(jnp.int32, dest.shape, 1)
    mine = dest == me
    first = jnp.min(jnp.where(mine, lane, dest.shape[1]), axis=1)
    last = jnp.max(jnp.where(mine, lane, -1), axis=1)
    place_first = jnp.sum(jnp.where(lane == first[:, None], pos, 0), axis=1)
    place_last = jnp.sum(jnp.where(lane == last[:, None], pos, 0), axis=1)
    place_first = jnp.where(last >= 0, place_first, blocks)
    place_last = jnp.where(last > first, place_last, blocks)
    return jnp.stack([place_first, place_last], axis=1).reshape(-1)


def per_device(front, pivot, panel, child_blocks, child_dest, child_pos, pattern):
    devices = lax.axis_size("row") * lax.axis_size("col")
    me = lax.axis_index("row") * lax.axis_size("col") + lax.axis_index("col")
    size = panel.shape[1]
    dest = child_dest[:, 0]
    outgoing = pack(dest, child_blocks, devices)
    notes = jnp.concatenate([dest[None], child_pos[None], jnp.zeros((6, dest.shape[0]), jnp.int32)], axis=0)
    everything = gather(jnp.concatenate([pivot, notes.astype(jnp.float32)], axis=1))
    outgoing, everything = lax.optimization_barrier((outgoing, everything))
    arrived = lax.all_to_all(outgoing, ("row", "col"), split_axis=0, concat_axis=0, tiled=True)
    factor, rounded = cholesky_solve(everything, panel)
    row_side, col_side = spread(rounded)
    told = everything[:, size:].reshape(devices, 8, -1).astype(jnp.int32)
    tile_blocks = (front.shape[0] // SIDE) * (front.shape[1] // SIDE)
    places = arrivals(told[:, 0], told[:, 1], me, tile_blocks)
    schur = finish(places, pattern, front, arrived, row_side, col_side)
    return (schur, factor)


def solution(mesh):
    return jax.shard_map(
        per_device,
        mesh=mesh,
        in_specs=(
            P("row", "col"),
            P(("row", "col"), None),
            P(("row", "col"), None),
            P(("row", "col"), None, None),
            P(("row", "col"), None),
            P(("row", "col")),
            P("row", "col"),
        ),
        out_specs=(P("row", "col"), P(("row", "col"), None)),
        check_vma=False,
    )
```

```python
import jax
import jax.numpy as jnp
from jax import lax
from jax.experimental import pallas as pl
from jax.experimental.pallas import tpu as pltpu
from jax.sharding import PartitionSpec as P

SIDE = 128
SUB = 8
HIGHEST = lax.Precision.HIGHEST
MESH = pl.DeviceIdType.MESH
VMEM = pltpu.VMEM
HBM = pltpu.HBM
CONTRACT_LAST = (((1,), (1,)), ((), ()))


def coordinates():
    row, col = lax.axis_index("row"), lax.axis_index("col")
    return {
        "y": row // 2,
        "x": (row % 2) * 2 + (col // 2) % 2,
        "z": col // 4,
        "core": col % 2,
    }


def mesh_index(at):
    return (at["y"] * 2 + at["x"] // 2, at["z"] * 4 + (at["x"] % 2) * 2 + at["core"])


def meet(peers, more=0):
    barrier = pltpu.get_barrier_semaphore()
    for peer in peers:
        pl.semaphore_signal(barrier, inc=1, device_id=peer, device_id_type=MESH)
    pl.semaphore_wait(barrier, len(peers) + more)


def pack_kernel(dest_ref, blocks_ref, out_ref, count, sem):
    devices = count.shape[0]
    number = blocks_ref.shape[0]

    @pl.loop(0, devices)
    def _(d):
        count[d] = 0

    @pl.loop(0, number)
    def _(i):
        owner = dest_ref[i]
        used = count[owner]
        count[owner] = used + 1
        pltpu.make_async_copy(blocks_ref.at[i], out_ref.at[owner * 2 + used], sem).start()

    pltpu.make_async_copy(blocks_ref, blocks_ref, sem).wait()


def pack(dest, blocks, devices):
    number, side, _ = blocks.shape
    return pl.pallas_call(
        pack_kernel,
        out_shape=jax.ShapeDtypeStruct((2 * devices, side, side), blocks.dtype),
        grid_spec=pltpu.PrefetchScalarGridSpec(
            num_scalar_prefetch=1,
            grid=(),
            in_specs=[pl.BlockSpec(memory_space=VMEM)],
            out_specs=pl.BlockSpec(memory_space=HBM),
            scratch_shapes=[pltpu.SMEM((devices,), jnp.int32), pltpu.SemaphoreType.DMA],
        ),
        name="pack",
    )(dest, blocks)


ORDERS = (("x", "y", "z"), ("y", "z", "x"), ("z", "x", "y"))
RING = 4


def gather_kernel(piece_bounds, own_ref, out_ref, local_sem, send_sem, recv_sem, ring_send, ring_recv, pair_send, pair_recv):
    me = coordinates()
    pieces = range(len(ORDERS))

    def view(piece, done, at, part=None):
        low, high = piece_bounds[piece] if part is None else part
        pick = lambda value, axis: slice(None) if axis in done else value
        return out_ref.at[
            pick(at["y"], "y"), pick(at["x"] // 2, "x"), pick(at["z"], "z"), pick(at["x"] % 2, "x"), me["core"],
            :, pl.ds(low, high - low),
        ]

    def moved(axis, value):
        at = dict(me)
        at[axis] = value
        return at

    copy = pltpu.make_async_copy(own_ref, out_ref.at[me["y"], me["x"] // 2, me["z"], me["x"] % 2, me["core"]], local_sem)
    copy.start()

    def send(piece, stage, turn):
        done, axis = ORDERS[piece][:stage], ORDERS[piece][stage]
        low, high = piece_bounds[piece]
        there = view(piece, done, me)
        return pltpu.make_async_remote_copy(
            src_ref=own_ref.at[:, pl.ds(low, high - low)] if stage == 0 else there,
            dst_ref=there,
            send_sem=send_sem.at[piece, stage, turn - 1],
            recv_sem=recv_sem.at[piece, stage, turn - 1],
            device_id=mesh_index(moved(axis, jnp.bitwise_xor(me[axis], turn))),
            device_id_type=MESH,
        )

    def ring(piece, step, turn):
        first, axis = ORDERS[piece][1:]
        low, high = piece_bounds[piece]
        cut = low + ((high - low) // SIDE * 2 // 3) * SIDE
        up, down = (me[axis] + 1) % RING, (me[axis] + RING - 1) % RING
        origin, target, part = (
            (me[axis], up, (low, high)), (me[axis], down, (low, high)), (down, up, (low, cut)), (up, down, (cut, high)),
        )[step]
        at = moved(axis, origin)
        at[first] = jnp.bitwise_xor(me[first], turn)
        ref = view(piece, ORDERS[piece][:1], at, part)
        return pltpu.make_async_remote_copy(
            src_ref=ref, dst_ref=ref, send_sem=ring_send.at[piece, step, turn], recv_sem=ring_recv.at[piece, step, turn],
            device_id=mesh_index(moved(axis, target)), device_id_type=MESH,
        )

    def pair(piece, step):
        done, axis = ORDERS[piece][:2], ORDERS[piece][2]
        ref = view(piece, done, moved(axis, (me[axis] + (0, RING - 1, 1, 2)[step]) % RING))
        return pltpu.make_async_remote_copy(
            src_ref=ref, dst_ref=ref, send_sem=pair_send.at[piece, step], recv_sem=pair_recv.at[piece, step],
            device_id=mesh_index(moved("core", 1 - me["core"])), device_id_type=MESH,
        )

    turns = (1, 3, 2)
    meet([mesh_index(moved(axis, jnp.bitwise_xor(me[axis], turn))) for axis in "xyz" for turn in turns]
         + [mesh_index(moved("core", 1 - me["core"]))])
    for piece in pieces:
        for turn in turns:
            send(piece, 0, turn).start()
    copy.wait()
    for piece in pieces:
        for turn in turns:
            send(piece, 0, turn).wait_recv()
        for turn in turns:
            send(piece, 1, turn).start()
        ring(piece, 0, 0).start()
        ring(piece, 1, 0).start()
    for turn in turns:
        for piece in pieces:
            send(piece, 1, turn).wait_recv()
            ring(piece, 0, turn).start()
            ring(piece, 1, turn).start()
    for piece in pieces:
        pair(piece, 0).start()
    for turn in (0, *turns):
        for piece in pieces:
            for step in (0, 1):
                ring(piece, step, turn).wait_recv()
                ring(piece, step + 2, turn).start()
    for piece in pieces:
        pair(piece, 1).start()
        pair(piece, 2).start()
    for piece in pieces:
        for turn in (0, *turns):
            ring(piece, 2, turn).wait_recv()
            ring(piece, 3, turn).wait_recv()
        pair(piece, 3).start()
    for piece in pieces:
        for turn in turns:
            send(piece, 0, turn).wait_send()
            send(piece, 1, turn).wait_send()
        for step in range(4):
            for turn in range(RING):
                ring(piece, step, turn).wait_send()
            pair(piece, step).wait()


def gather(own):
    rows, width = own.shape
    third = (width // SIDE // 3) * SIDE
    bounds = ((0, third), (third, 2 * third), (2 * third, width))
    count = len(ORDERS)
    dma = pltpu.SemaphoreType.DMA

    def kernel(*refs):
        gather_kernel(bounds, *refs)

    out = pl.pallas_call(
        kernel,
        out_shape=jax.ShapeDtypeStruct((4, 2, 4, 2, 2, rows, width), own.dtype),
        in_specs=[pl.BlockSpec(memory_space=HBM)],
        out_specs=pl.BlockSpec(memory_space=HBM),
        scratch_shapes=[
            dma, dma((count, 2, 3)), dma((count, 2, 3)), dma((count, 4, RING)), dma((count, 4, RING)), dma((count, 4)), dma((count, 4)),
        ],
        compiler_params=pltpu.CompilerParams(has_side_effects=True, collective_id=0),
        name="pivot_gather",
    )(own)
    return out.reshape(128 * rows, width)


def factor_block(load, store):
    groups = SIDE // SUB
    block = [load(h) for h in range(groups)]
    rows = lax.broadcasted_iota(jnp.int32, (SUB, SIDE), 0)
    cols = lax.broadcasted_iota(jnp.int32, (SUB, SIDE), 1)
    inverse = [jnp.where(cols == rows + SUB * h, 1.0, 0.0).astype(jnp.float32) for h in range(groups)]

    def spread_row(value, r):
        return jnp.broadcast_to(value[r : r + 1, :], (SUB, SIDE))

    def spread_column(value, c):
        return jnp.broadcast_to(value[:, c : c + 1], (SUB, SIDE))

    for g in range(groups):
        heads = [spread_column(block[g], SUB * g + j) for j in range(SUB)]
        corner = {(i, j): spread_row(heads[j], i) for j in range(SUB) for i in range(j, SUB)}
        upper = [spread_row(block[g], i) for i in range(SUB)]
        lower = [spread_row(inverse[g], i) for i in range(SUB)]
        below = {h: [spread_column(block[h], SUB * g + j) for j in range(SUB)] for h in range(g + 1, groups)}
        for j in range(SUB):
            scale = lax.rsqrt(corner[j, j])
            column = {i: corner[i, j] * scale for i in range(j + 1, SUB)}
            for i in range(j + 1, SUB):
                for k in range(j + 1, i + 1):
                    corner[i, k] = corner[i, k] - column[i] * column[k]
            u = upper[j] * scale
            w = lower[j] * scale
            for i in range(j + 1, SUB):
                upper[i] = upper[i] - column[i] * u
                lower[i] = lower[i] - column[i] * w
            for h in range(g + 1, groups):
                entry = below[h][j] * scale
                for i in range(j + 1, SUB):
                    below[h][i] = below[h][i] - entry * column[i]
                block[h] = block[h] - entry * u
                inverse[h] = inverse[h] - entry * w
            store(SUB * g + j, w[0:1, :])


def cholesky_kernel(pivot_ref, panel_ref, factor_ref, rounded_ref, work, solved, inverse):
    size = factor_ref.shape[1]
    own = panel_ref.shape[0]
    blocks = size // SIDE
    work[pl.ds(0, size), :] = pivot_ref[:, pl.ds(0, size)]
    work[pl.ds(size, own), :] = panel_ref[...]

    @pl.loop(0, blocks)
    def _(k):
        start = pl.multiple_of(k * SIDE, SIDE)
        columns = pl.ds(start, SIDE)

        def load(h):
            return work[pl.ds(pl.multiple_of(start + SUB * h, SUB), SUB), columns]

        def store(r, value):
            inverse[r : r + 1, :] = value

        factor_block(load, store)
        solved[...] = lax.dot_general(
            work[:, columns], inverse[...], CONTRACT_LAST, precision=HIGHEST, preferred_element_type=jnp.float32
        )
        mine = solved[pl.ds(size, own), :]
        factor_ref[:, columns] = mine
        rounded_ref[:, columns] = mine.astype(jnp.bfloat16)

        @pl.loop(k + 1, blocks)
        def _(j):
            there = pl.multiple_of(j * SIDE, SIDE)
            work[:, pl.ds(there, SIDE)] = work[:, pl.ds(there, SIDE)] - lax.dot_general(
                solved[...], solved[pl.ds(there, SIDE), :], CONTRACT_LAST,
                precision=HIGHEST, preferred_element_type=jnp.float32,
            )


def cholesky_solve(pivot, panel):
    own, size = panel.shape
    return pl.pallas_call(
        cholesky_kernel,
        out_shape=(jax.ShapeDtypeStruct((own, size), jnp.float32), jax.ShapeDtypeStruct((own, size), jnp.bfloat16)),
        in_specs=[pl.BlockSpec(memory_space=VMEM)] * 2,
        out_specs=(pl.BlockSpec(memory_space=VMEM),) * 2,
        scratch_shapes=[
            VMEM((size + own, size), jnp.float32), VMEM((size + own, SIDE), jnp.float32), VMEM((SIDE, SIDE), jnp.float32),
        ],
        compiler_params=pltpu.CompilerParams(vmem_limit_bytes=30 << 20),
        cost_estimate=pl.CostEstimate(flops=10**10, bytes_accessed=10**7, transcendentals=0),
        name="cholesky_solve",
    )(pivot, panel)


def spread_kernel(
    own_ref, row_ref, col_ref, local_sem, turn_send, turn_recv, send_sem, recv_sem, pair_send, pair_recv,
):
    me = coordinates()
    core = me["core"]
    row, chip = lax.axis_index("row"), lax.axis_index("col") // 2
    parts = turn_send.shape[0]
    width = own_ref.shape[1] // parts
    sides = (
        (row_ref, "z", me["x"] % 2, lambda flip: me["x"] // 2 * 2 + flip),
        (col_ref, "y", me["x"] // 2, lambda flip: flip * 2 + me["x"] % 2),
    )

    def moved(axis, value):
        at = dict(me)
        at[axis] = value
        return mesh_index(at)

    shifts = ((0, 0), (chip // 2, chip % 2))

    def slot(side, place, flip):
        return jnp.bitwise_xor(place, shifts[side][0]), jnp.bitwise_xor(sides[side][2], jnp.bitwise_xor(shifts[side][1], flip))

    def block(side, place, flip):
        high, low = slot(side, place, flip)
        return sides[side][0].at[high, low, core]

    def cut(ref, q):
        return ref.at[:, pl.ds(q * width, width)]

    def send(side, kind, q):
        _, axis, mine, place_x = sides[side]
        here = me[axis]
        up, down = (here + 1) % RING, (here + RING - 1) % RING
        if kind == 0:
            origin, flip, target = here, 0, moved("x", place_x(1 - mine))
        elif kind < 5:
            origin, flip, target = here, (kind - 1) // 2, moved(axis, (up, down)[(kind - 1) % 2])
        else:
            origin, flip, target = (down, up)[q % 2], kind - 5, moved(axis, (up, down)[q % 2])
        ref = block(side, origin, flip)
        return pltpu.make_async_remote_copy(
            src_ref=cut(own_ref if side == 0 and kind < 3 else ref, q), dst_ref=cut(ref, q),
            send_sem=send_sem.at[side, kind, q], recv_sem=recv_sem.at[side, kind, q],
            device_id=target, device_id_type=MESH,
        )

    def pair(side, shift, flip):
        place = (me[sides[side][1]] + shift) % RING
        ref = block(side, place, flip)
        go = pltpu.make_async_remote_copy(
            src_ref=own_ref if side == 0 and shift == 0 and flip == 0 else ref, dst_ref=ref,
            send_sem=pair_send.at[side], recv_sem=pair_recv.at[side],
            device_id=moved("core", 1 - core), device_id_type=MESH,
        )
        if side == 0:
            go.start()
        else:
            @pl.when(slot(side, place, flip)[0] // 2 != core)
            def _():
                go.start()

    turned = col_ref.at[chip // 2, chip % 2, core]
    stay = pltpu.make_async_copy(own_ref, turned, local_sem.at[1])
    across = (jnp.bitwise_xor(row, chip), row * 2 + core)
    source = (chip, jnp.bitwise_xor(row, chip) * 2 + core)
    at_home = jnp.logical_and(row == 0, chip == 0)

    def turn(q):
        return pltpu.make_async_remote_copy(
            src_ref=cut(own_ref, q), dst_ref=cut(turned, q), send_sem=turn_send.at[q], recv_sem=turn_recv.at[q],
            device_id=across, device_id_type=MESH,
        )

    barrier = pltpu.get_barrier_semaphore()

    @pl.when(jnp.logical_not(at_home))
    def _():
        pl.semaphore_signal(barrier, inc=1, device_id=source, device_id_type=MESH)

    peers = [moved("core", 1 - core)]
    for _, axis, mine, place_x in sides:
        peers += [moved(axis, (me[axis] + 1) % RING), moved(axis, (me[axis] + RING - 1) % RING), moved("x", place_x(1 - mine))]
    meet(peers, jnp.where(at_home, 0, 1))
    local = pltpu.make_async_copy(own_ref, row_ref.at[me["z"], me["x"] % 2, core], local_sem.at[0])
    local.start()

    @pl.when(at_home)
    def _():
        stay.start()

    @pl.when(jnp.logical_not(at_home))
    def _():
        for q in range(parts):
            turn(q).start()

    for q in range(parts):
        for kind in (0, 1, 2):
            send(0, kind, q).start()
    pair(0, 0, 0)

    @pl.when(at_home)
    def _():
        stay.wait()

    for q in range(parts):
        @pl.when(jnp.logical_not(at_home))
        def _():
            turn(q).wait_recv()

        for kind in (0, 1, 2):
            send(1, kind, q).start()
    pair(1, 0, 0)
    for flip in (0, 1):
        for q in range(parts):
            for side in (0, 1):
                if flip == 0:
                    send(side, 0, q).wait_recv()
                    send(side, 3, q).start()
                    send(side, 4, q).start()
                send(side, 1 + 2 * flip + q % 2, q).wait_recv()
                send(side, 5 + flip, q).start()
    for flip in (0, 1):
        for side in (0, 1):
            if flip == 0:
                pair(side, 0, 1)
            for q in range(parts):
                send(side, 2 + 2 * flip - q % 2, q).wait_recv()
            pair(side, RING - 1, flip)
            pair(side, 1, flip)
            for q in range(parts):
                send(side, 5 + flip, q).wait_recv()
            pair(side, 2, flip)
    local.wait()

    @pl.when(jnp.logical_not(at_home))
    def _():
        for q in range(parts):
            turn(q).wait_send()

    for side in (0, 1):
        for kind in range(7):
            for q in range(parts):
                send(side, kind, q).wait_send()
        ref = sides[side][0].at[pl.ds(0, RING if side == 0 else 2), :, 0]
        whole = pltpu.make_async_remote_copy(
            src_ref=ref, dst_ref=ref, send_sem=pair_send.at[side], recv_sem=pair_recv.at[side],
            device_id=moved("core", 1 - core), device_id_type=MESH,
        )
        whole.wait()


def spread(rounded):
    own, size = rounded.shape
    dma = pltpu.SemaphoreType.DMA
    side = jax.ShapeDtypeStruct((RING, 2, 2, own, size), rounded.dtype)
    parts = 4
    row_side, col_side = pl.pallas_call(
        spread_kernel,
        out_shape=(side, side),
        in_specs=[pl.BlockSpec(memory_space=VMEM)],
        out_specs=(pl.BlockSpec(memory_space=SPREAD_SPACE),) * 2,
        scratch_shapes=[
            dma((2,)), dma((parts,)), dma((parts,)), dma((2, 7, parts)), dma((2, 7, parts)), dma((2,)), dma((2,)),
        ],
        compiler_params=pltpu.CompilerParams(has_side_effects=True, collective_id=1, vmem_limit_bytes=SPREAD_LIMIT),
        name="factor_spread",
    )(rounded)
    return row_side.reshape(16 * own, size), col_side.reshape(16 * own, size)


SPREAD_SPACE = HBM
SPREAD_LIMIT = 62 << 20


UNROLL = 4


def finish_kernel(
    slot_ref, place_ref, start_ref, pattern_ref, front_ref, arrived_ref, row_ref, col_ref, out_ref,
    tile, product, slots, rows, cols, front_sem, slot_sem, row_sem, col_sem, out_sem,
):
    bands = out_sem.shape[0]
    full, width = product.shape
    height = full // bands
    chunk = slots.shape[0] // bands
    block_cols = width // SIDE
    blocks = (full // SIDE) * block_cols
    core = lax.axis_index("col") % 2

    def band(b):
        return pl.ds(pl.multiple_of(b * height, height), height)

    def part(b):
        return pl.ds(b * chunk, chunk)

    half = pl.ds(pl.multiple_of(core * width, SIDE), width)
    load_cols = pltpu.make_async_copy(col_ref.at[half], cols, col_sem)

    def load_front(b):
        return pltpu.make_async_copy(front_ref.at[band(b)], tile.at[band(b)], front_sem.at[b])

    def load_rows(b):
        return pltpu.make_async_copy(row_ref.at[band(b)], rows.at[band(b)], row_sem.at[b])

    def load_slots(b):
        return pltpu.make_async_copy(arrived_ref.at[part(b)], slots.at[part(b)], slot_sem.at[b])

    def put(b):
        return pltpu.make_async_copy(tile.at[band(b)], out_ref.at[band(b)], out_sem.at[b])

    load_cols.start()
    for b in range(bands):
        load_rows(b).start()
    load_cols.wait()
    for b in range(bands):
        load_rows(b).wait()
    for load in (load_slots, load_front):
        for b in range(bands):
            load(b).start()

    @pl.loop(0, bands)
    def _(b):
        value = lax.dot_general(rows[band(b), :], cols[...], CONTRACT_LAST, preferred_element_type=jnp.float32)
        for i in range(height // SIDE):
            for j in range(block_cols):
                keep = pattern_ref[b * (height // SIDE) + i, j].astype(jnp.float32)
                here = (pl.ds(pl.multiple_of(b * height + i * SIDE, SIDE), SIDE), pl.ds(j * SIDE, SIDE))
                product[here] = value[i * SIDE : (i + 1) * SIDE, j * SIDE : (j + 1) * SIDE] * keep

    for b in range(bands):
        load_slots(b).wait()

    @pl.loop(0, bands)
    def _(b):
        load_front(b).wait()
        low, high = start_ref[b], start_ref[b + 1]

        @pl.loop(0, (high - low + UNROLL - 1) // UNROLL)
        def _(t):
            for n in range(UNROLL):
                entry = low + t * UNROLL + n
                place = jnp.where(entry < high, place_ref[entry], blocks)
                top = pl.multiple_of((place // block_cols) * SIDE, SIDE)
                left = pl.multiple_of((place % block_cols) * SIDE, SIDE)
                here = (pl.ds(top, SIDE), pl.ds(left, SIDE))
                tile[here] = tile[here] + slots[slot_ref[entry]].astype(jnp.float32)

        tile[band(b), :] = tile[band(b), :] - product[band(b), :]
        put(b).start()

    @pl.loop(0, bands)
    def _(b):
        put(b).wait()


def finish(plan, pattern, front, arrived, row_side, col_side):
    dma = pltpu.SemaphoreType.DMA
    height, width = front.shape
    size = row_side.shape[1]
    bands = height // BAND
    return pl.pallas_call(
        finish_kernel,
        out_shape=jax.ShapeDtypeStruct(front.shape, front.dtype),
        grid_spec=pltpu.PrefetchScalarGridSpec(
            num_scalar_prefetch=4,
            grid=(),
            in_specs=[pl.BlockSpec(memory_space=HBM)] * 4,
            out_specs=pl.BlockSpec(memory_space=HBM),
            scratch_shapes=[
                VMEM((height + SIDE, width), jnp.float32), VMEM(front.shape, jnp.float32),
                VMEM(arrived.shape, arrived.dtype), VMEM(row_side.shape, row_side.dtype), VMEM((width, size), col_side.dtype),
                dma((bands,)), dma((bands,)), dma((bands,)), dma, dma((bands,)),
            ],
        ),
        compiler_params=pltpu.CompilerParams(vmem_limit_bytes=62 << 20),
        name="finish",
    )(*plan, pattern, front, arrived, row_side, col_side)


BAND = 256


def arrivals(dest, pos, me, tile_rows, tile_cols):
    block_cols = tile_cols // SIDE
    blocks = (tile_rows // SIDE) * block_cols
    lane = lax.broadcasted_iota(jnp.int32, dest.shape, 1)
    mine = dest == me
    first = jnp.min(jnp.where(mine, lane, dest.shape[1]), axis=1)
    last = jnp.max(jnp.where(mine, lane, -1), axis=1)
    place_first = jnp.sum(jnp.where(lane == first[:, None], pos, 0), axis=1)
    place_last = jnp.sum(jnp.where(lane == last[:, None], pos, 0), axis=1)
    place_first = jnp.where(last >= 0, place_first, blocks)
    place_last = jnp.where(last > first, place_last, blocks)
    count = dest.shape[0]
    number = jnp.arange(count, dtype=jnp.int32)
    place = jnp.concatenate([place_first, place_last])
    key = place * (2 * count) + jnp.concatenate([2 * number, 2 * number + 1])
    rank = jnp.sum((key[:, None] > key[None, :]).astype(jnp.int32), axis=1)
    at = rank[None, :] == jnp.arange(2 * count, dtype=jnp.int32)[:, None]
    ordered = jnp.sum(jnp.where(at, key[None, :], 0), axis=1)
    edges = jnp.arange(tile_rows // BAND + 1, dtype=jnp.int32) * (BAND // SIDE * block_cols)
    starts = jnp.sum((place[None, :] < edges[:, None]).astype(jnp.int32), axis=1)
    spare = jnp.full((UNROLL,), blocks * 2 * count, jnp.int32)
    ordered = jnp.concatenate([ordered, spare])
    return ordered % (2 * count), ordered // (2 * count), starts


def per_device(front, pivot, panel, child_blocks, child_dest, child_pos, pattern):
    devices = lax.axis_size("row") * lax.axis_size("col")
    me = lax.axis_index("row") * lax.axis_size("col") + lax.axis_index("col")
    size = panel.shape[1]
    dest = child_dest[:, 0]
    outgoing = pack(dest, child_blocks, devices)
    notes = jnp.concatenate([dest[None], child_pos[None], jnp.zeros((6, dest.shape[0]), jnp.int32)], axis=0)
    everything = gather(jnp.concatenate([pivot, notes.astype(jnp.float32)], axis=1))
    outgoing, everything = lax.optimization_barrier((outgoing, everything))
    arrived = lax.all_to_all(outgoing, ("row", "col"), split_axis=0, concat_axis=0, tiled=True)
    told = everything[:, size:].reshape(devices, 8, -1).astype(jnp.int32)
    plan = arrivals(told[:, 0], told[:, 1], me, *front.shape)
    panel, plan, pattern = lax.optimization_barrier((panel, plan, pattern))
    factor, rounded = cholesky_solve(everything, panel)
    row_side, col_side = spread(rounded)
    schur = finish(plan, pattern, front, arrived, row_side, col_side)
    return (schur, factor)


def solution(mesh):
    return jax.shard_map(
        per_device,
        mesh=mesh,
        in_specs=(
            P("row", "col"),
            P(("row", "col"), None),
            P(("row", "col"), None),
            P(("row", "col"), None, None),
            P(("row", "col"), None),
            P(("row", "col")),
            P("row", "col"),
        ),
        out_specs=(P("row", "col"), P(("row", "col"), None)),
        check_vma=False,
    )
```

```python
import jax
import jax.numpy as jnp
from jax import lax
from jax.experimental import pallas as pl
from jax.experimental.pallas import tpu as pltpu
from jax.sharding import PartitionSpec as P

SIDE = 128
SUB = 8
HIGHEST = lax.Precision.HIGHEST
MESH = pl.DeviceIdType.MESH
VMEM = pltpu.VMEM
HBM = pltpu.HBM
CONTRACT_LAST = (((1,), (1,)), ((), ()))


def coordinates():
    row, col = lax.axis_index("row"), lax.axis_index("col")
    return {
        "y": row // 2,
        "x": (row % 2) * 2 + (col // 2) % 2,
        "z": col // 4,
        "core": col % 2,
    }


def mesh_index(at):
    return (at["y"] * 2 + at["x"] // 2, at["z"] * 4 + (at["x"] % 2) * 2 + at["core"])


def meet(peers, more=0):
    barrier = pltpu.get_barrier_semaphore()
    for peer in peers:
        pl.semaphore_signal(barrier, inc=1, device_id=peer, device_id_type=MESH)
    pl.semaphore_wait(barrier, len(peers) + more)


def pack_kernel(dest_ref, blocks_ref, out_ref, blocks, count, load_sem, sem):
    devices = count.shape[0]
    chunks = load_sem.shape[0]
    chunk = blocks.shape[0] // chunks

    def load(c):
        part = pl.ds(c * chunk, chunk)
        return pltpu.make_async_copy(blocks_ref.at[part], blocks.at[part], load_sem.at[c])

    for c in range(chunks):
        load(c).start()

    @pl.loop(0, devices)
    def _(d):
        count[d] = 0

    for c in range(chunks):
        load(c).wait()

        @pl.loop(c * chunk, (c + 1) * chunk)
        def _(i):
            owner = dest_ref[i]
            used = count[owner]
            count[owner] = used + 1
            pltpu.make_async_copy(blocks.at[i], out_ref.at[owner * 2 + used], sem).start()

    pltpu.make_async_copy(blocks, blocks, sem).wait()


def pack(dest, blocks, devices):
    number, side, _ = blocks.shape
    dma = pltpu.SemaphoreType.DMA
    return pl.pallas_call(
        pack_kernel,
        out_shape=jax.ShapeDtypeStruct((2 * devices, side, side), blocks.dtype),
        grid_spec=pltpu.PrefetchScalarGridSpec(
            num_scalar_prefetch=1,
            grid=(),
            in_specs=[pl.BlockSpec(memory_space=HBM)],
            out_specs=pl.BlockSpec(memory_space=HBM),
            scratch_shapes=[VMEM(blocks.shape, blocks.dtype), pltpu.SMEM((devices,), jnp.int32), dma((4,)), dma],
        ),
        compiler_params=pltpu.CompilerParams(vmem_limit_bytes=62 << 20),
        name="pack",
    )(dest, blocks)


ORDERS = (("x", "y", "z"), ("y", "z", "x"), ("z", "x", "y"))
RING = 4
NOTED = 128


def gather_kernel(pivot_ref, notes_ref, *refs):
    outs, (local_sem, send_sem, recv_sem, ring_send, ring_recv, pair_send, pair_recv) = refs[:3], refs[3:]
    me = coordinates()
    pieces = range(len(ORDERS))
    width = outs[0].shape[-1]
    rest = pivot_ref.shape[1] - 2 * width
    core = me["core"]

    def moved(axis, value):
        at = dict(me)
        at[axis] = value
        return at

    def places(piece):
        return tuple(me[axis] for axis in ORDERS[piece])

    def send(piece, stage, turn):
        first, second, last = places(piece)
        axis = ORDERS[piece][stage]
        ref = outs[piece].at[core, last, second, first] if stage == 0 else outs[piece].at[core, last, second]
        return pltpu.make_async_remote_copy(
            src_ref=ref, dst_ref=ref,
            send_sem=send_sem.at[piece, stage, turn - 1], recv_sem=recv_sem.at[piece, stage, turn - 1],
            device_id=mesh_index(moved(axis, jnp.bitwise_xor(me[axis], turn))), device_id_type=MESH,
        )

    def ring(piece, step, turn):
        _, second, last = places(piece)
        axis = ORDERS[piece][2]
        up, down = (last + 1) % RING, (last + RING - 1) % RING
        origin, target = ((last, up), (last, down), (down, up), (up, down))[step]
        ref = outs[piece].at[core, origin, jnp.bitwise_xor(second, turn)]
        if step >= 2:
            ref = ref.at[pl.ds((step - 2) * 2, 2)]
        return pltpu.make_async_remote_copy(
            src_ref=ref, dst_ref=ref, send_sem=ring_send.at[piece, step, turn], recv_sem=ring_recv.at[piece, step, turn],
            device_id=mesh_index(moved(axis, target)), device_id_type=MESH,
        )

    def pair(piece, step):
        last = places(piece)[2]
        ref = outs[piece].at[core, (last + (0, RING - 1, 1, 2)[step]) % RING]
        return pltpu.make_async_remote_copy(
            src_ref=ref, dst_ref=ref, send_sem=pair_send.at[piece, step], recv_sem=pair_recv.at[piece, step],
            device_id=mesh_index(moved("core", 1 - core)), device_id_type=MESH,
        )

    def own(piece):
        first, second, last = places(piece)
        return outs[piece].at[core, last, second, first]

    copies = (
        pltpu.make_async_copy(pivot_ref.at[:, pl.ds(0, width)], own(0), local_sem.at[0]),
        pltpu.make_async_copy(pivot_ref.at[:, pl.ds(width, width)], own(1), local_sem.at[1]),
        pltpu.make_async_copy(pivot_ref.at[:, pl.ds(2 * width, rest)], own(2).at[:, pl.ds(0, rest)], local_sem.at[2]),
        pltpu.make_async_copy(notes_ref, own(2).at[:, pl.ds(rest, NOTED)], local_sem.at[3]),
    )
    for copy in copies:
        copy.start()
    turns = (1, 3, 2)
    meet([mesh_index(moved(axis, jnp.bitwise_xor(me[axis], turn))) for axis in "xyz" for turn in turns]
         + [mesh_index(moved("core", 1 - core))])
    for copy in copies:
        copy.wait()
    for piece in pieces:
        for turn in turns:
            send(piece, 0, turn).start()
    for piece in pieces:
        for turn in turns:
            send(piece, 0, turn).wait_recv()
        for turn in turns:
            send(piece, 1, turn).start()
        ring(piece, 0, 0).start()
        ring(piece, 1, 0).start()
    for turn in turns:
        for piece in pieces:
            send(piece, 1, turn).wait_recv()
            ring(piece, 0, turn).start()
            ring(piece, 1, turn).start()
    for piece in pieces:
        pair(piece, 0).start()
    for turn in (0, *turns):
        for piece in pieces:
            for step in (0, 1):
                ring(piece, step, turn).wait_recv()
                ring(piece, step + 2, turn).start()
    for piece in pieces:
        pair(piece, 1).start()
        pair(piece, 2).start()
    for piece in pieces:
        for turn in (0, *turns):
            ring(piece, 2, turn).wait_recv()
            ring(piece, 3, turn).wait_recv()
        pair(piece, 3).start()
    for piece in pieces:
        for turn in turns:
            send(piece, 0, turn).wait_send()
            send(piece, 1, turn).wait_send()
        for step in range(4):
            for turn in range(RING):
                ring(piece, step, turn).wait_send()
            pair(piece, step).wait()


def gather(pivot, notes):
    rows, width = pivot.shape[0], (pivot.shape[1] + NOTED) // 3
    count = len(ORDERS)
    dma = pltpu.SemaphoreType.DMA
    return pl.pallas_call(
        gather_kernel,
        out_shape=(jax.ShapeDtypeStruct((2, RING, RING, RING, rows, width), pivot.dtype),) * 3,
        in_specs=[pl.BlockSpec(memory_space=VMEM)] * 2,
        out_specs=(pl.BlockSpec(memory_space=HBM),) * 3,
        scratch_shapes=[
            dma((4,)), dma((count, 2, 3)), dma((count, 2, 3)), dma((count, 4, RING)), dma((count, 4, RING)), dma((count, 4)), dma((count, 4)),
        ],
        compiler_params=pltpu.CompilerParams(has_side_effects=True, collective_id=0, vmem_limit_bytes=62 << 20),
        name="pivot_gather",
    )(pivot, notes)


def factor_block(load, store):
    groups = SIDE // SUB
    block = [load(h) for h in range(groups)]
    rows = lax.broadcasted_iota(jnp.int32, (SUB, SIDE), 0)
    cols = lax.broadcasted_iota(jnp.int32, (SUB, SIDE), 1)
    inverse = [jnp.where(cols == rows + SUB * h, 1.0, 0.0).astype(jnp.float32) for h in range(groups)]

    def spread_row(value, r):
        return jnp.broadcast_to(value[r : r + 1, :], (SUB, SIDE))

    def spread_column(value, c):
        return jnp.broadcast_to(value[:, c : c + 1], (SUB, SIDE))

    for g in range(groups):
        heads = [spread_column(block[g], SUB * g + j) for j in range(SUB)]
        corner = {(i, j): spread_row(heads[j], i) for j in range(SUB) for i in range(j, SUB)}
        upper = [spread_row(block[g], i) for i in range(SUB)]
        lower = [spread_row(inverse[g], i) for i in range(SUB)]
        below = {h: [spread_column(block[h], SUB * g + j) for j in range(SUB)] for h in range(g + 1, groups)}
        for j in range(SUB):
            scale = lax.rsqrt(corner[j, j])
            column = {i: corner[i, j] * scale for i in range(j + 1, SUB)}
            for i in range(j + 1, SUB):
                for k in range(j + 1, i + 1):
                    corner[i, k] = corner[i, k] - column[i] * column[k]
            u = upper[j] * scale
            w = lower[j] * scale
            for i in range(j + 1, SUB):
                upper[i] = upper[i] - column[i] * u
                lower[i] = lower[i] - column[i] * w
            for h in range(g + 1, groups):
                entry = below[h][j] * scale
                for i in range(j + 1, SUB):
                    below[h][i] = below[h][i] - entry * column[i]
                block[h] = block[h] - entry * u
                inverse[h] = inverse[h] - entry * w
            store(SUB * g + j, w[0:1, :])


def cholesky_kernel(left_ref, middle_ref, right_ref, panel_ref, factor_ref, rounded_ref, work, solved, inverse):
    size = factor_ref.shape[1]
    own = panel_ref.shape[0]
    blocks = size // SIDE

    @pl.loop(0, size // SUB)
    def _(d):
        row, col = d // 16, d % 16
        at = {"y": row // 2, "x": (row % 2) * 2 + (col // 2) % 2, "z": col // 4}
        here = pl.ds(pl.multiple_of(d * SUB, SUB), SUB)
        for piece, ref in enumerate((left_ref, middle_ref, right_ref)):
            first, second, last = (at[axis] for axis in ORDERS[piece])
            low = piece * ref.shape[-1]
            keep = min(ref.shape[-1], size - low)
            work[here, pl.ds(low, keep)] = ref[col % 2, last, second, first, :, pl.ds(0, keep)]

    work[pl.ds(size, own), :] = panel_ref[...]

    @pl.loop(0, blocks)
    def _(k):
        start = pl.multiple_of(k * SIDE, SIDE)
        columns = pl.ds(start, SIDE)

        def load(h):
            return work[pl.ds(pl.multiple_of(start + SUB * h, SUB), SUB), columns]

        def store(r, value):
            inverse[r : r + 1, :] = value

        factor_block(load, store)
        solved[...] = lax.dot_general(
            work[:, columns], inverse[...], CONTRACT_LAST, precision=HIGHEST, preferred_element_type=jnp.float32
        )
        mine = solved[pl.ds(size, own), :]
        factor_ref[:, columns] = mine
        rounded_ref[:, columns] = mine.astype(jnp.bfloat16)

        @pl.loop(k + 1, blocks)
        def _(j):
            there = pl.multiple_of(j * SIDE, SIDE)
            work[:, pl.ds(there, SIDE)] = work[:, pl.ds(there, SIDE)] - lax.dot_general(
                solved[...], solved[pl.ds(there, SIDE), :], CONTRACT_LAST,
                precision=HIGHEST, preferred_element_type=jnp.float32,
            )


def cholesky_solve(pieces, panel):
    own, size = panel.shape
    return pl.pallas_call(
        cholesky_kernel,
        out_shape=(jax.ShapeDtypeStruct((own, size), jnp.float32), jax.ShapeDtypeStruct((own, size), jnp.bfloat16)),
        in_specs=[pl.BlockSpec(memory_space=VMEM)] * 4,
        out_specs=(pl.BlockSpec(memory_space=VMEM),) * 2,
        scratch_shapes=[
            VMEM((size + own, size), jnp.float32), VMEM((size + own, SIDE), jnp.float32), VMEM((SIDE, SIDE), jnp.float32),
        ],
        compiler_params=pltpu.CompilerParams(vmem_limit_bytes=30 << 20),
        cost_estimate=pl.CostEstimate(flops=10**10, bytes_accessed=10**7, transcendentals=0),
        name="cholesky_solve",
    )(*pieces, panel)


def spread_kernel(
    own_ref, row_ref, col_ref, local_sem, turn_send, turn_recv, send_sem, recv_sem, pair_send, pair_recv,
):
    me = coordinates()
    core = me["core"]
    row, chip = lax.axis_index("row"), lax.axis_index("col") // 2
    parts = turn_send.shape[0]
    width = own_ref.shape[1] // parts
    sides = (
        (row_ref, "z", me["x"] % 2, lambda flip: me["x"] // 2 * 2 + flip),
        (col_ref, "y", me["x"] // 2, lambda flip: flip * 2 + me["x"] % 2),
    )

    def moved(axis, value):
        at = dict(me)
        at[axis] = value
        return mesh_index(at)

    shifts = ((0, 0), (chip // 2, chip % 2))

    def slot(side, place, flip):
        return jnp.bitwise_xor(place, shifts[side][0]), jnp.bitwise_xor(sides[side][2], jnp.bitwise_xor(shifts[side][1], flip))

    def block(side, place, flip):
        high, low = slot(side, place, flip)
        return sides[side][0].at[high, low, core]

    def cut(ref, q):
        return ref.at[:, pl.ds(q * width, width)]

    def send(side, kind, q):
        _, axis, mine, place_x = sides[side]
        here = me[axis]
        up, down = (here + 1) % RING, (here + RING - 1) % RING
        if kind == 0:
            origin, flip, target = here, 0, moved("x", place_x(1 - mine))
        elif kind < 5:
            origin, flip, target = here, (kind - 1) // 2, moved(axis, (up, down)[(kind - 1) % 2])
        else:
            origin, flip, target = (down, up)[q % 2], kind - 5, moved(axis, (up, down)[q % 2])
        ref = block(side, origin, flip)
        return pltpu.make_async_remote_copy(
            src_ref=cut(own_ref if side == 0 and kind < 3 else ref, q), dst_ref=cut(ref, q),
            send_sem=send_sem.at[side, kind, q], recv_sem=recv_sem.at[side, kind, q],
            device_id=target, device_id_type=MESH,
        )

    def pair(side, shift, flip):
        place = (me[sides[side][1]] + shift) % RING
        ref = block(side, place, flip)
        go = pltpu.make_async_remote_copy(
            src_ref=own_ref if side == 0 and shift == 0 and flip == 0 else ref, dst_ref=ref,
            send_sem=pair_send.at[side], recv_sem=pair_recv.at[side],
            device_id=moved("core", 1 - core), device_id_type=MESH,
        )
        if side == 0:
            go.start()
        else:
            @pl.when(slot(side, place, flip)[0] // 2 != core)
            def _():
                go.start()

    turned = col_ref.at[chip // 2, chip % 2, core]
    stay = pltpu.make_async_copy(own_ref, turned, local_sem.at[1])
    across = (jnp.bitwise_xor(row, chip), row * 2 + core)
    source = (chip, jnp.bitwise_xor(row, chip) * 2 + core)
    at_home = jnp.logical_and(row == 0, chip == 0)

    def turn(q):
        return pltpu.make_async_remote_copy(
            src_ref=cut(own_ref, q), dst_ref=cut(turned, q), send_sem=turn_send.at[q], recv_sem=turn_recv.at[q],
            device_id=across, device_id_type=MESH,
        )

    barrier = pltpu.get_barrier_semaphore()

    @pl.when(jnp.logical_not(at_home))
    def _():
        pl.semaphore_signal(barrier, inc=1, device_id=source, device_id_type=MESH)

    peers = [moved("core", 1 - core)]
    for _, axis, mine, place_x in sides:
        peers += [moved(axis, (me[axis] + 1) % RING), moved(axis, (me[axis] + RING - 1) % RING), moved("x", place_x(1 - mine))]
    meet(peers, jnp.where(at_home, 0, 1))
    local = pltpu.make_async_copy(own_ref, row_ref.at[me["z"], me["x"] % 2, core], local_sem.at[0])
    local.start()

    @pl.when(at_home)
    def _():
        stay.start()

    @pl.when(jnp.logical_not(at_home))
    def _():
        for q in range(parts):
            turn(q).start()

    for q in range(parts):
        for kind in (0, 1, 2):
            send(0, kind, q).start()
    pair(0, 0, 0)

    @pl.when(at_home)
    def _():
        stay.wait()

    for q in range(parts):
        @pl.when(jnp.logical_not(at_home))
        def _():
            turn(q).wait_recv()

        for kind in (0, 1, 2):
            send(1, kind, q).start()
    pair(1, 0, 0)
    for flip in (0, 1):
        for q in range(parts):
            for side in (0, 1):
                if flip == 0:
                    send(side, 0, q).wait_recv()
                    send(side, 3, q).start()
                    send(side, 4, q).start()
                send(side, 1 + 2 * flip + q % 2, q).wait_recv()
                send(side, 5 + flip, q).start()
    for flip in (0, 1):
        for side in (0, 1):
            if flip == 0:
                pair(side, 0, 1)
            for q in range(parts):
                send(side, 2 + 2 * flip - q % 2, q).wait_recv()
            pair(side, RING - 1, flip)
            pair(side, 1, flip)
            for q in range(parts):
                send(side, 5 + flip, q).wait_recv()
            pair(side, 2, flip)
    local.wait()

    @pl.when(jnp.logical_not(at_home))
    def _():
        for q in range(parts):
            turn(q).wait_send()

    for side in (0, 1):
        for kind in range(7):
            for q in range(parts):
                send(side, kind, q).wait_send()
        ref = sides[side][0].at[pl.ds(0, RING if side == 0 else 2), :, 0]
        whole = pltpu.make_async_remote_copy(
            src_ref=ref, dst_ref=ref, send_sem=pair_send.at[side], recv_sem=pair_recv.at[side],
            device_id=moved("core", 1 - core), device_id_type=MESH,
        )
        whole.wait()


def spread(rounded):
    own, size = rounded.shape
    dma = pltpu.SemaphoreType.DMA
    side = jax.ShapeDtypeStruct((RING, 2, 2, own, size), rounded.dtype)
    parts = 4
    row_side, col_side = pl.pallas_call(
        spread_kernel,
        out_shape=(side, side),
        in_specs=[pl.BlockSpec(memory_space=VMEM)],
        out_specs=(pl.BlockSpec(memory_space=SPREAD_SPACE),) * 2,
        scratch_shapes=[
            dma((2,)), dma((parts,)), dma((parts,)), dma((2, 7, parts)), dma((2, 7, parts)), dma((2,)), dma((2,)),
        ],
        compiler_params=pltpu.CompilerParams(has_side_effects=True, collective_id=1, vmem_limit_bytes=SPREAD_LIMIT),
        name="factor_spread",
    )(rounded)
    return row_side.reshape(16 * own, size), col_side.reshape(16 * own, size)


SPREAD_SPACE = HBM
SPREAD_LIMIT = 62 << 20


UNROLL = 4


def finish_kernel(
    slot_ref, place_ref, start_ref, pattern_ref, front_ref, arrived_ref, row_ref, col_ref, out_ref,
    tile, product, slots, rows, cols, front_sem, slot_sem, row_sem, col_sem, out_sem,
):
    bands = out_sem.shape[0]
    full, width = product.shape
    height = full // bands
    chunk = slots.shape[0] // bands
    block_cols = width // SIDE
    blocks = (full // SIDE) * block_cols
    core = lax.axis_index("col") % 2

    def band(b):
        return pl.ds(pl.multiple_of(b * height, height), height)

    def part(b):
        return pl.ds(b * chunk, chunk)

    half = pl.ds(pl.multiple_of(core * width, SIDE), width)
    load_cols = pltpu.make_async_copy(col_ref.at[half], cols, col_sem)

    def load_front(b):
        return pltpu.make_async_copy(front_ref.at[band(b)], tile.at[band(b)], front_sem.at[b])

    def load_rows(b):
        return pltpu.make_async_copy(row_ref.at[band(b)], rows.at[band(b)], row_sem.at[b])

    def load_slots(b):
        return pltpu.make_async_copy(arrived_ref.at[part(b)], slots.at[part(b)], slot_sem.at[b])

    def put(b):
        return pltpu.make_async_copy(tile.at[band(b)], out_ref.at[band(b)], out_sem.at[b])

    load_cols.start()
    for b in range(bands):
        load_rows(b).start()
    load_cols.wait()
    for b in range(bands):
        load_rows(b).wait()
    for load in (load_slots, load_front):
        for b in range(bands):
            load(b).start()

    @pl.loop(0, bands)
    def _(b):
        value = lax.dot_general(rows[band(b), :], cols[...], CONTRACT_LAST, preferred_element_type=jnp.float32)
        for i in range(height // SIDE):
            for j in range(block_cols):
                keep = pattern_ref[b * (height // SIDE) + i, j].astype(jnp.float32)
                here = (pl.ds(pl.multiple_of(b * height + i * SIDE, SIDE), SIDE), pl.ds(j * SIDE, SIDE))
                product[here] = value[i * SIDE : (i + 1) * SIDE, j * SIDE : (j + 1) * SIDE] * keep

    for b in range(bands):
        load_slots(b).wait()

    @pl.loop(0, bands)
    def _(b):
        load_front(b).wait()
        low, high = start_ref[b], start_ref[b + 1]

        @pl.loop(0, (high - low + UNROLL - 1) // UNROLL)
        def _(t):
            for n in range(UNROLL):
                entry = low + t * UNROLL + n
                place = jnp.where(entry < high, place_ref[entry], blocks)
                top = pl.multiple_of((place // block_cols) * SIDE, SIDE)
                left = pl.multiple_of((place % block_cols) * SIDE, SIDE)
                here = (pl.ds(top, SIDE), pl.ds(left, SIDE))
                tile[here] = tile[here] + slots[slot_ref[entry]].astype(jnp.float32)

        tile[band(b), :] = tile[band(b), :] - product[band(b), :]
        put(b).start()

    @pl.loop(0, bands)
    def _(b):
        put(b).wait()


def finish(plan, pattern, front, arrived, row_side, col_side):
    dma = pltpu.SemaphoreType.DMA
    height, width = front.shape
    size = row_side.shape[1]
    bands = height // BAND
    return pl.pallas_call(
        finish_kernel,
        out_shape=jax.ShapeDtypeStruct(front.shape, front.dtype),
        grid_spec=pltpu.PrefetchScalarGridSpec(
            num_scalar_prefetch=4,
            grid=(),
            in_specs=[pl.BlockSpec(memory_space=HBM)] * 4,
            out_specs=pl.BlockSpec(memory_space=HBM),
            scratch_shapes=[
                VMEM((height + SIDE, width), jnp.float32), VMEM(front.shape, jnp.float32),
                VMEM(arrived.shape, arrived.dtype), VMEM(row_side.shape, row_side.dtype), VMEM((width, size), col_side.dtype),
                dma((bands,)), dma((bands,)), dma((bands,)), dma, dma((bands,)),
            ],
        ),
        compiler_params=pltpu.CompilerParams(vmem_limit_bytes=62 << 20),
        name="finish",
    )(*plan, pattern, front, arrived, row_side, col_side)


BAND = 256


def arrivals(dest, pos, me, tile_rows, tile_cols):
    block_cols = tile_cols // SIDE
    blocks = (tile_rows // SIDE) * block_cols
    lane = lax.broadcasted_iota(jnp.int32, dest.shape, 1)
    mine = dest == me
    first = jnp.min(jnp.where(mine, lane, dest.shape[1]), axis=1)
    last = jnp.max(jnp.where(mine, lane, -1), axis=1)
    place_first = jnp.sum(jnp.where(lane == first[:, None], pos, 0), axis=1)
    place_last = jnp.sum(jnp.where(lane == last[:, None], pos, 0), axis=1)
    place_first = jnp.where(last >= 0, place_first, blocks)
    place_last = jnp.where(last > first, place_last, blocks)
    count = dest.shape[0]
    number = jnp.arange(count, dtype=jnp.int32)
    place = jnp.concatenate([place_first, place_last])
    key = place * (2 * count) + jnp.concatenate([2 * number, 2 * number + 1])
    rank = jnp.sum((key[:, None] > key[None, :]).astype(jnp.int32), axis=1)
    at = rank[None, :] == jnp.arange(2 * count, dtype=jnp.int32)[:, None]
    ordered = jnp.sum(jnp.where(at, key[None, :], 0), axis=1)
    edges = jnp.arange(tile_rows // BAND + 1, dtype=jnp.int32) * (BAND // SIDE * block_cols)
    starts = jnp.sum((place[None, :] < edges[:, None]).astype(jnp.int32), axis=1)
    spare = jnp.full((UNROLL,), blocks * 2 * count, jnp.int32)
    ordered = jnp.concatenate([ordered, spare])
    return ordered % (2 * count), ordered // (2 * count), starts


def per_device(front, pivot, panel, child_blocks, child_dest, child_pos, pattern):
    devices = lax.axis_size("row") * lax.axis_size("col")
    me = lax.axis_index("row") * lax.axis_size("col") + lax.axis_index("col")
    dest = child_dest[:, 0]
    outgoing = pack(dest, child_blocks, devices)
    notes = jnp.concatenate([dest[None], child_pos[None], jnp.zeros((6, dest.shape[0]), jnp.int32)], axis=0)
    everything = gather(pivot, notes.astype(jnp.float32))
    outgoing, everything = lax.optimization_barrier((outgoing, everything))
    arrived = lax.all_to_all(outgoing, ("row", "col"), split_axis=0, concat_axis=0, tiled=True)
    told = everything[2][..., :2, -NOTED:].reshape(2, 4, 2, 2, 4, 2, NOTED)
    told = told.transpose(5, 1, 2, 4, 3, 0, 6).reshape(2, devices, NOTED).astype(jnp.int32)
    plan = arrivals(told[0], told[1], me, *front.shape)
    panel, plan, pattern = lax.optimization_barrier((panel, plan, pattern))
    factor, rounded = cholesky_solve(everything, panel)
    row_side, col_side = spread(rounded)
    schur = finish(plan, pattern, front, arrived, row_side, col_side)
    return (schur, factor)


def solution(mesh):
    return jax.shard_map(
        per_device,
        mesh=mesh,
        in_specs=(
            P("row", "col"),
            P(("row", "col"), None),
            P(("row", "col"), None),
            P(("row", "col"), None, None),
            P(("row", "col"), None),
            P(("row", "col")),
            P("row", "col"),
        ),
        out_specs=(P("row", "col"), P(("row", "col"), None)),
        check_vma=False,
    )
```
